256 devices in a mesh: sector: 16 (over y, x_hi, core), depth: 16 (over x_lo, z).
Axes of the slice: x: 4 (x_hi: 2, x_lo: 2; x = x_hi * 2 + x_lo), y: 4, z: 8, core: 2. Of those that a mesh axis runs over, the one named last changes fastest.
Arguments:
- panel: bfloat16 [1048576, 128], P(('sector', 'depth')), may hold values from -6 to 6
- coords: int32 [3, 1048576], P(None, ('sector', 'depth')), may hold values from 0 to 127, as said below
- neighbours: int32 [8192, 32], P(('sector', 'depth')), may hold values from 0 to 8191, as said below
- ranges: float32 [3], replicated, may hold values from 6 to 20
Outputs:
- basis: float32 [1048576, 128], P(('sector', 'depth'))
- factor: float32 [128, 128], replicated
The draws below stay inside these ranges and needn't reach their ends.
Inputs may be any that keep to these rules, and one draw needn't show every extreme that they name: `coords`: each device's 32 * 128 cells occupy every point of its own grid box exactly once: azimuth columns s * 8 to (s + 1) * 8 - 1 for sector s, radial rows 0 to 63, depth layers d * 8 to (d + 1) * 8 - 1 for slab d, in an arbitrary order; cell blocks are numbered sector-major, then slab, then block. `neighbours`: each row lists 32 different block columns, all of the row's depth slab and of sectors at most two away from its own around the cycle.
All inputs are finite; a program needn't handle non-finite values.
Results may differ from the reference program's by a relative error of at most 0.0065.
Values may be sent and summed in bfloat16 or wider, within the bound.
A program may use at most 128 MiB of HBM per device.

```python
import jax
import jax.numpy as jnp
from jax import lax

BS = 128
RANK = 128
NNZ = 32
BLK_DEV = 32
AZ_SEC = 8
DZ = 8
SECTORS = 16
SLABS = 16
NAZ = 128
CELLS = 1048576
NBLOCKS = 8192


def draw_coords(key, part):
    per_device = BLK_DEV * BS
    devices = SECTORS * SLABS
    keys = jax.random.split(jax.random.fold_in(key, 11), devices)
    orders = jax.vmap(lambda single: jax.random.permutation(single, per_device))(keys).astype(jnp.int32)
    device = jnp.arange(devices, dtype=jnp.int32)[:, None]
    sector_id = device // SLABS
    slab_id = device % SLABS
    column = orders % AZ_SEC
    rest = orders // AZ_SEC
    layer = rest % DZ
    radial = rest // DZ
    azimuth = sector_id * AZ_SEC + column
    vertical = slab_id * DZ + layer
    return jnp.stack([azimuth.reshape(-1), radial.reshape(-1), vertical.reshape(-1)]).astype(jnp.int32)


def draw_neighbours(key, part):
    keys = jax.random.split(jax.random.fold_in(key, 23), NBLOCKS)
    chosen = jax.vmap(lambda single: jax.random.permutation(single, 5 * BLK_DEV))(keys)[:, :NNZ].astype(jnp.int32)
    block_row = jnp.arange(NBLOCKS, dtype=jnp.int32)[:, None]
    sector_id = block_row // (SLABS * BLK_DEV)
    slab_id = block_row // BLK_DEV % SLABS
    step_away = chosen // BLK_DEV - 2
    within = chosen % BLK_DEV
    target = (sector_id + step_away) % SECTORS * SLABS + slab_id
    return (target * BLK_DEV + within).astype(jnp.int32)


def shard_levels(own_key, shape, cuts, smallest, top_value):
    loudness, own = 1.0, jax.random.fold_in(own_key, 6)
    for position, shards_of in cuts:
        steps = jnp.exp(jax.random.uniform(jax.random.fold_in(own, position), (shards_of,), jnp.float32, smallest / len(cuts), top_value / len(cuts)))
        loudness = loudness * jnp.repeat(steps, shape[position] // shards_of).reshape([-1 if axis == position else 1 for axis in range(len(shape))])
    return loudness


def bell_draw(rng, extent, spread, most, cuts=(), held_as=jnp.bfloat16):
    values = jax.random.normal(rng, extent, jnp.float32) * spread
    if len(cuts) > 0:
        values = shard_levels(rng, extent, cuts, -0.22, 0.18) * values
    return jnp.clip(values, min=-most, max=most).astype(held_as)


def setup_inputs(seed: int = 0) -> dict:
    splits = jax.random.split(jax.random.key(seed), 5)
    return {
        "panel": bell_draw(splits[0], (CELLS, RANK), 1.0, 6.0, ((0, 256),)),
        "coords": draw_coords(jax.random.fold_in(splits[4], 71), 0),
        "neighbours": draw_neighbours(jax.random.fold_in(splits[4], 71), 0),
        "ranges": jnp.clip(jax.random.uniform(splits[3], (3,), jnp.float32, 6.0, 20.0), 6.0, 20.0),
    }


CUTOFF = 3.0
NUGGET = 0.5

def cov_blocks(home, remote, ranges, period):
    diffs = (home[:, None, :, :, None] - remote[:, :, :, None, :]).astype(jnp.float32)
    along = jnp.abs(diffs[:, :, 0])
    along = jnp.minimum(along, period - along)
    scaled = (along / ranges[0]) ** 2 + (diffs[:, :, 1] / ranges[1]) ** 2 + (diffs[:, :, 2] / ranges[2]) ** 2
    radius = jnp.sqrt(scaled)
    taper = jnp.maximum(1.0 - radius / CUTOFF, 0.0)
    weight = 8.0 / jnp.sqrt(jnp.float32(remote.shape[1] * remote.shape[3]))
    return (weight * jnp.exp(-radius) * taper * taper).astype(jnp.bfloat16)

def reference(panel, coords, neighbours, ranges):
    blocked = panel.reshape(NBLOCKS, BS, RANK)
    cell_coords = jnp.transpose(coords.reshape(3, NBLOCKS, BS), (1, 0, 2))
    group = 32
    period = jnp.float32(NAZ)

    def one_group(inputs):
        rows_coords, rows_panel, rows_list = inputs
        remote_coords = cell_coords[rows_list]
        remote_panel = blocked[rows_list]
        kernel = cov_blocks(rows_coords, remote_coords, ranges, period)
        product = jnp.einsum('gnab,gnbc->gac', kernel.astype(jnp.float32), remote_panel.astype(jnp.float32), precision=lax.Precision.HIGHEST)
        return product + NUGGET * rows_panel.astype(jnp.float32)
    image = lax.map(one_group, (cell_coords.reshape(NBLOCKS // group, group, 3, BS), blocked.reshape(NBLOCKS // group, group, BS, RANK), neighbours.reshape(NBLOCKS // group, group, NNZ)))
    image = image.reshape(CELLS, RANK)
    gram = jnp.dot(image.T.astype(jnp.float32), image.astype(jnp.float32), precision=lax.Precision.HIGHEST, preferred_element_type=jnp.float32) / jnp.float32(CELLS)
    lower = jnp.linalg.cholesky(gram)
    inverse = jax.scipy.linalg.solve_triangular(lower, jnp.eye(RANK, dtype=jnp.float32), lower=True)
    basis = jnp.dot(image.astype(jnp.float32), inverse.T.astype(jnp.float32), precision=lax.Precision.HIGHEST, preferred_element_type=jnp.float32)
    return (basis, lower.T)
```

```python
import functools

import jax
import jax.numpy as jnp
from jax import lax
from jax.experimental import pallas as pl
from jax.experimental.pallas import tpu as pltpu
from jax.sharding import PartitionSpec as P

AZ_SEC = 8
DZ = 8
CUTOFF = 3.0
NUGGET = 0.5
BS = 128
LOG2E = 1.4426950408889634
MESH = pl.DeviceIdType.MESH
F32 = jnp.float32
BF16 = jnp.bfloat16
HIGHEST = lax.Precision.HIGHEST


def passed_along(block, axis, distance):
    devices = range(lax.axis_size(axis))
    route = [((i - distance) % len(devices), i) for i in devices]
    return lax.ppermute(block, axis, route)


def pieces(value):
    one = lax.reduce_precision(value, 8, 7)
    two = lax.reduce_precision(value - one, 8, 7)
    three = value - one - two
    return one, two, three


def image_kernel(cols, left_ref, right_ref, panel_ref, own_ref, image_ref, gram_ref):
    rows = left_ref.shape[0]
    slots = cols.shape[1]
    rank = panel_ref.shape[2]
    gram_ref[...] = jnp.zeros_like(gram_ref)

    def one_row(g, carry):
        left = left_ref[g]
        acc = jnp.zeros((BS, rank), F32)
        for n in range(0, slots, 2):
            ha = cols[g, n]
            hb = cols[g, n + 1]
            right = jnp.concatenate([right_ref[ha], right_ref[hb]], axis=1)
            square = jnp.dot(left, right, preferred_element_type=F32)
            square = jnp.maximum(square, 1e-12)
            reach = square * lax.rsqrt(square)
            decay = jnp.exp2(reach * (-CUTOFF * LOG2E))
            taper = jnp.maximum(1.0 - reach, 0.0)
            block = (decay * taper * taper).astype(BF16)
            parts = jnp.concatenate([panel_ref[ha], panel_ref[hb]], axis=0)
            acc = acc + jnp.dot(block, parts, preferred_element_type=F32)
        image = acc * 0.125 + NUGGET * own_ref[g].astype(F32)
        image_ref[g] = image
        high = image.astype(BF16)
        low = (image - high.astype(F32)).astype(BF16)
        both = jnp.concatenate([high, low], axis=1)
        gram_ref[...] += lax.dot_general(
            high, both, (((0,), (0,)), ((), ())), preferred_element_type=F32
        )
        return carry

    lax.fori_loop(0, rows, one_row, 0)


def image_and_gram(cols, left, right, panel, own):
    rows = left.shape[0]
    rank = panel.shape[2]
    vmem = pl.BlockSpec(memory_space=pltpu.VMEM)
    return pl.pallas_call(
        image_kernel,
        name="image",
        out_shape=(
            jax.ShapeDtypeStruct((rows, BS, rank), F32),
            jax.ShapeDtypeStruct((rank, 2 * rank), F32),
        ),
        in_specs=[pl.BlockSpec(memory_space=pltpu.SMEM), vmem, vmem, vmem, vmem],
        out_specs=(vmem, vmem),
        compiler_params=pltpu.CompilerParams(vmem_limit_bytes=48 << 20),
    )(cols, left, right, panel, own)


def place():
    s = lax.axis_index("sector")
    d = lax.axis_index("depth")
    return s // 4, (s // 2) % 2, s % 2, d // 8, d % 8


def all_sum_kernel(total, part_ref, out_ref, got1, got2, got3, mine, whole, s1, r1, s2, r2, s3, r3):
    y, xh, core, xl, z = place()
    q = core * 8 + z
    r = y * 4 + xh * 2 + xl

    def peer_q(k):
        p = lax.rem(q + k, 16)
        return p, (y * 4 + xh * 2 + p // 8, xl * 8 + lax.rem(p, 8))

    def peer_r(k):
        p = lax.rem(r + k, 16)
        return p, ((p // 2) * 2 + core, lax.rem(p, 2) * 8 + z)

    barrier = pltpu.get_barrier_semaphore()

    def greet(k, c):
        pl.semaphore_signal(barrier, inc=1, device_id=peer_q(k)[1], device_id_type=MESH)
        pl.semaphore_signal(barrier, inc=1, device_id=peer_r(k)[1], device_id_type=MESH)
        return c

    lax.fori_loop(1, 16, greet, 0)
    pl.semaphore_wait(barrier, 30)

    def copy1(k):
        p, dev = peer_q(k)
        return pltpu.make_async_remote_copy(
            part_ref.at[p], got1.at[q], s1.at[k], r1.at[k], device_id=dev, device_id_type=MESH
        )

    def copy2(k):
        dev = peer_r(k)[1]
        return pltpu.make_async_remote_copy(
            mine, got2.at[r], s2.at[k], r2.at[k], device_id=dev, device_id_type=MESH
        )

    def copy3(k):
        dev = peer_q(k)[1]
        return pltpu.make_async_remote_copy(
            whole, got3.at[q], s3.at[k], r3.at[k], device_id=dev, device_id_type=MESH
        )

    def start(copy):
        def step(k, c):
            copy(k).start()
            return c

        lax.fori_loop(1, 16, step, 0)

    def arrive(copy):
        def step(k, c):
            copy(k).wait_recv()
            return c

        lax.fori_loop(1, 16, step, 0)

    def leave(copy):
        def step(k, c):
            copy(k).wait_send()
            return c

        lax.fori_loop(1, 16, step, 0)

    start(copy1)
    got1[q] = part_ref[q]
    arrive(copy1)
    mine[...] = jnp.sum(got1[...], axis=0)
    start(copy2)
    got2[r] = mine[...]
    arrive(copy2)
    whole[...] = jnp.sum(got2[...], axis=0) * (1.0 / total)
    start(copy3)
    got3[q] = whole[...]
    arrive(copy3)
    out_ref[...] = got3[...]
    leave(copy1)
    leave(copy2)
    leave(copy3)


def all_sum(part, total):
    vmem = pl.BlockSpec(memory_space=pltpu.VMEM)
    rank = part.shape[1]
    rows = part.shape[0] // 16
    out = pl.pallas_call(
        functools.partial(all_sum_kernel, total),
        name="all_sum",
        out_shape=jax.ShapeDtypeStruct((16, rows, rank), F32),
        in_specs=[vmem],
        out_specs=vmem,
        scratch_shapes=[pltpu.VMEM((16, rows, rank), F32)] * 3
        + [pltpu.VMEM((rows, rank), F32)] * 2
        + [pltpu.SemaphoreType.DMA((16,))] * 6,
        compiler_params=pltpu.CompilerParams(collective_id=1, has_side_effects=True),
    )(part.reshape(16, rows, rank))
    return out.reshape(part.shape)


def nt(a, b):
    return lax.dot_general(
        a, b, (((1,), (1,)), ((), ())), precision=HIGHEST, preferred_element_type=F32
    )


def nn(a, b):
    return jnp.dot(a, b, precision=HIGHEST, preferred_element_type=F32)


def basis_kernel(gram_ref, image_ref, basis_ref, factor_ref, inverse_ref, work_ref):
    n = gram_ref.shape[0]

    @pl.when(pl.program_id(0) == 0)
    def _():
        row = lax.broadcasted_iota(jnp.int32, (n, n), 0)
        col = lax.broadcasted_iota(jnp.int32, (n, n), 1)
        diag = row == col
        weight = jnp.where(row > col, 1.0, jnp.where(diag, 0.5, 0.0)).astype(F32)
        eye = jnp.where(diag, 1.0, 0.0).astype(F32)
        gram = gram_ref[...]
        only = jnp.where(diag, gram, 0.0)
        down = lax.rsqrt(jnp.sum(only, axis=1, keepdims=True))
        across = lax.rsqrt(jnp.sum(only, axis=0, keepdims=True))
        first = gram * down * across - eye
        inverse_ref[...] = (eye - first * weight) * across

        def unsettled(state):
            size, turn = state
            return jnp.logical_and(jnp.logical_not(size < 1e-6), turn < 8)

        def refine(state):
            turn = state[1]
            x = inverse_ref[...]
            gap = nt(nn(x, gram_ref[...]), x) - eye
            inverse_ref[...] = x - nn(gap * weight, x)
            return jnp.sum(gap * gap), turn + 1

        size, _ = lax.while_loop(unsettled, refine, (jnp.sum(first * first), jnp.int32(0)))
        settled = size < 1e-6

        @pl.when(settled)
        def _():
            factor_ref[...] = jnp.where(row <= col, nn(inverse_ref[...], gram_ref[...]), 0.0)

        @pl.when(jnp.logical_not(settled))
        def _():
            work_ref[:, :n] = gram_ref[...]
            work_ref[:, n:] = eye
            wide = lax.broadcasted_iota(jnp.int32, (n, 2 * n), 1)
            tall = lax.broadcasted_iota(jnp.int32, (n, 1), 0)

            def eliminate(k, c):
                m = work_ref[...]
                pivot_row = jnp.sum(jnp.where(tall == k, m, 0.0), axis=0, keepdims=True)
                column = jnp.sum(jnp.where(wide == k, m, 0.0), axis=1, keepdims=True)
                pivot = jnp.sum(jnp.where(tall == k, column, 0.0), axis=0, keepdims=True)
                ratio = jnp.where(tall > k, column / pivot, 0.0)
                work_ref[...] = m - ratio * pivot_row
                return c

            lax.fori_loop(0, n, eliminate, 0)
            upper = work_ref[:, :n]
            scale = lax.rsqrt(jnp.sum(jnp.where(diag, upper, 0.0), axis=1, keepdims=True))
            factor_ref[...] = jnp.where(row <= col, upper * scale, 0.0)
            inverse_ref[...] = work_ref[:, n:] * scale

    x = inverse_ref[...]
    xh = x.astype(BF16)
    xl = (x - xh.astype(F32)).astype(BF16)
    image = image_ref[...]
    high = image.astype(BF16)
    low = (image - high.astype(F32)).astype(BF16)

    def times(a, b):
        return lax.dot_general(a, b, (((1,), (1,)), ((), ())), preferred_element_type=F32)

    basis_ref[...] = times(high, xh) + times(high, xl) + times(low, xh)


def basis_and_factor(gram, image):
    n = gram.shape[0]
    rows = image.shape[0]
    step = 512
    return pl.pallas_call(
        basis_kernel,
        name="basis",
        grid=(rows // step,),
        out_shape=(
            jax.ShapeDtypeStruct((rows, n), F32),
            jax.ShapeDtypeStruct((n, n), F32),
        ),
        in_specs=[
            pl.BlockSpec((n, n), lambda i: (0, 0)),
            pl.BlockSpec((step, n), lambda i: (i, 0)),
        ],
        out_specs=(
            pl.BlockSpec((step, n), lambda i: (i, 0)),
            pl.BlockSpec((n, n), lambda i: (0, 0)),
        ),
        scratch_shapes=[pltpu.VMEM((n, n), F32), pltpu.VMEM((n, 2 * n), F32)],
    )(gram, image)


def on_device(panel, coords, neighbours, ranges):
    block_count = neighbours.shape[0]
    block_size = panel.shape[0] // block_count
    width = panel.shape[1]
    sector_count = lax.axis_size("sector")
    slab_count = lax.axis_size("depth")
    my_sector = lax.axis_index("sector")
    my_slab = lax.axis_index("depth")
    blocked = panel.reshape(block_count, block_size, width)

    low = jnp.stack([my_sector * AZ_SEC, 32, my_slab * DZ + DZ // 2]).astype(jnp.int32)
    inside = (coords - low[:, None]).astype(BF16)
    near = {d: passed_along((blocked, inside), "sector", d) for d in (1, -1)}
    far = {d: passed_along(near[d], "sector", d) for d in (1, -1)}
    ordered = [far[1], near[1], (blocked, inside), near[-1], far[-1]]
    wide_panel = jnp.concatenate([member[0] for member in ordered], axis=0)

    scale = 1.0 / (ranges * CUTOFF) ** 2
    remote = []
    for step, member in enumerate(ordered):
        shift = jnp.array([8.0 * (step - 2) - 4.0, 0.0, 0.0], F32)
        place3 = member[1].astype(F32) + shift[:, None]
        norm = jnp.sum(scale[:, None] * place3 * place3, axis=0)
        n1, n2, n3 = pieces(norm)
        one = jnp.ones_like(norm)
        zero = jnp.zeros_like(norm)
        rows = jnp.concatenate(
            [place3, place3, place3, jnp.stack([one, one, one, n1, n2, n3, zero])], axis=0
        )
        remote.append(rows.reshape(16, block_count, block_size))
        if step == 2:
            a1, a2, a3 = pieces(-2.0 * scale[:, None] * place3)
            home = jnp.concatenate(
                [a1, a2, a3, jnp.stack([n1, n2, n3, one, one, one, zero])], axis=0
            )
            home = home.astype(BF16).reshape(16, block_count, block_size)
    right = jnp.transpose(jnp.concatenate(remote, axis=1).astype(BF16), (1, 0, 2))
    left = jnp.transpose(home, (1, 2, 0))

    column_sector = neighbours // (slab_count * block_count)
    step_away = (column_sector - my_sector + 2) % sector_count
    local_column = step_away * block_count + neighbours % block_count

    image, gram2 = image_and_gram(local_column, left, right, wide_panel, blocked)
    cross = gram2[:, width:]
    part = gram2[:, :width] + cross + cross.T
    image = image.reshape(block_count * block_size, width)
    total_cells = float(image.shape[0] * sector_count * slab_count)
    gram = all_sum(part, total_cells)
    basis, factor = basis_and_factor(gram, image)
    return (basis, factor)


def solution(mesh):
    in_specs = (
        P(("sector", "depth"), None),
        P(None, ("sector", "depth")),
        P(("sector", "depth"), None),
        P(),
    )
    out_specs = (P(("sector", "depth"), None), P())
    return jax.shard_map(
        on_device, mesh=mesh, in_specs=in_specs, out_specs=out_specs, check_vma=False
    )
```

```python
import functools
import math

import jax
import jax.numpy as jnp
from jax import lax
from jax.experimental import pallas as pl
from jax.experimental.pallas import tpu as pltpu
from jax.sharding import PartitionSpec as P

AZ_SEC = 8
DZ = 8
CUTOFF = 3.0
NUGGET = 0.5
BS = 128
LOG2E = 1.4426950408889634
MESH = pl.DeviceIdType.MESH
F32 = jnp.float32
BF16 = jnp.bfloat16
HIGHEST = lax.Precision.HIGHEST


STEPS = 5


def place():
    s = lax.axis_index("sector")
    d = lax.axis_index("depth")
    return s // 4, (s // 2) % 2, s % 2, d // 8, d % 8


def short(value):
    return value.astype(BF16).astype(F32)


def pieces(value):
    one = short(value)
    two = short(value - one)
    return one, two, value - one - two


def image_kernel(
    total, cols, scale, mine_ref, own_ref, image_ref, gram_ref,
    block_ref, wide_ref, place_ref, right_ref, left_ref, local_ref,
    part_ref, got1, got2, got3, mine, whole,
    place_s, place_r, cross_s, cross_r, along_s, along_r, twin_s, twin_r, own_s, own_r,
    s1, r1, s2, r2, s3, r3,
):
    rows, rank = own_ref.shape[0], own_ref.shape[2]
    slots = cols.shape[1]
    chunks = cross_s.shape[0]
    size = rows // chunks
    y, xh, core, xl, z = place()
    s = lax.axis_index("sector")
    d = lax.axis_index("depth")
    q = core * 8 + z
    r = y * 4 + xh * 2 + xl

    def sector(k):
        return lax.rem(s + k + 16, 16), d

    def peer_q(k):
        p = lax.rem(q + k, 16)
        return p, (y * 4 + xh * 2 + p // 8, xl * 8 + lax.rem(p, 8))

    def peer_r(k):
        p = lax.rem(r + k, 16)
        return p, ((p // 2) * 2 + core, lax.rem(p, 2) * 8 + z)

    barrier = pltpu.get_barrier_semaphore()
    for k in (-2, -1, 1, 2, -4, 4):
        pl.semaphore_signal(barrier, inc=1, device_id=sector(k), device_id_type=MESH)

    def greet(k, c):
        pl.semaphore_signal(barrier, inc=1, device_id=peer_q(k)[1], device_id_type=MESH)
        pl.semaphore_signal(barrier, inc=1, device_id=peer_r(k)[1], device_id_type=MESH)
        return c

    lax.fori_loop(1, 16, greet, 0)
    pl.semaphore_wait(barrier, 36)

    opposite = sector(2 - 4 * xh)
    onward = sector(4 - 8 * xh)
    across_at = (4 - 4 * xh) * rows
    along_at = 4 * xh * rows
    twin = sector(1 - 2 * core)
    twin_from = (4 - 4 * core) * rows
    twin_to = (3 - 2 * core) * rows
    own_to = (1 + 2 * core) * rows

    def remote(src, dst, send, recv, dev):
        return pltpu.make_async_remote_copy(
            src, dst, send, recv, device_id=dev, device_id_type=MESH
        )

    def place_copy(i):
        k = (-2, -1, 1, 2)[i]
        return remote(mine_ref, place_ref.at[2 - k], place_s.at[i], place_r.at[i], sector(k))

    def cross_copy(c):
        return remote(
            own_ref.at[pl.ds(c * size, size)],
            wide_ref.at[pl.ds(4 * xh * rows + c * size, size)],
            cross_s.at[c], cross_r.at[c], opposite,
        )

    def along_copy(c):
        return remote(
            wide_ref.at[pl.ds(across_at + c * size, size)],
            wide_ref.at[pl.ds(along_at + c * size, size)],
            along_s.at[c], along_r.at[c], onward,
        )

    def twin_copy(c):
        return remote(
            wide_ref.at[pl.ds(twin_from + c * size, size)],
            wide_ref.at[pl.ds(twin_to + c * size, size)],
            twin_s.at[c], twin_r.at[c], twin,
        )

    def own_copy():
        return remote(own_ref, wide_ref.at[pl.ds(own_to, rows)], own_s, own_r, twin)

    def every(count, do):
        def step(k, c):
            do(k)
            return c

        lax.fori_loop(0, count, step, 0)

    for i in range(4):
        place_copy(i).start()
    every(chunks, lambda c: cross_copy(c).start())
    own_copy().start()
    wide_ref[pl.ds(2 * rows, rows)] = own_ref[...]
    local_ref[...] = jnp.zeros_like(local_ref)

    line = lax.broadcasted_iota(jnp.int32, (1, 8, BS), 1)
    w = jnp.where(line == 0, scale[0], jnp.where(line == 1, scale[1], scale[2]))
    w = jnp.where(line < 3, w, 0.0)

    def spread(ref_value, step):
        even = ref_value.astype(F32).reshape(rows // 2, 8, BS)
        odd = jnp.concatenate([even[:, 4:], even[:, :4]], axis=1)
        both = jnp.stack([even, odd], axis=1).reshape(rows, 8, BS)
        both = both + jnp.where(line == 0, 8.0 * (step - 2) - 4.0, 0.0)
        norm = jnp.sum(both * both * w, axis=1, keepdims=True)
        return both, norm

    def put_right(both, norm, step):
        n1, n2, n3 = pieces(norm)
        tail = jnp.where(line == 4, n1, jnp.where(line == 5, n2, jnp.where(line == 6, n3, 0.0)))
        base = jnp.where(line < 4, both, tail)
        twice = jnp.concatenate([base, base], axis=1).astype(BF16)
        right_ref[pl.ds(step * rows, rows)] = twice

    both, norm = spread(mine_ref[...], 2)
    put_right(both, norm, 2)
    full = jnp.where(line < 3, -2.0 * w * both, jnp.where(line == 3, norm, 0.0))
    a1, a2, a3 = pieces(full)
    a1 = a1 + jnp.where(jnp.logical_and(line > 3, line < 7), 1.0, 0.0)
    left_ref[...] = jnp.concatenate([a1, a2, a3, jnp.zeros_like(a1)], axis=1)
    for i in range(4):
        place_copy(i).wait_recv()
    for step in (0, 1, 3, 4):
        both, norm = spread(place_ref[step], step)
        put_right(both, norm, step)

    def build(g):
        left = jnp.transpose(left_ref[g]).astype(BF16)
        for n in range(0, slots, 2):
            right = jnp.concatenate([right_ref[cols[g, n]], right_ref[cols[g, n + 1]]], axis=1)
            right = jnp.concatenate([right, right], axis=0)
            square = jnp.dot(left, right, preferred_element_type=F32)
            square = jnp.maximum(square, 1e-10)
            rest = CUTOFF * LOG2E - square * lax.rsqrt(square)
            taper = jnp.maximum(rest, 0.0)
            block = jnp.exp2(rest) * taper * taper
            block_ref[g, :, n * BS : (n + 2) * BS] = block.astype(BF16)

    lag = 2

    def turn(c, carry):
        every(size, lambda i: build(c * size + i))
        cross_copy(c).wait_recv()
        along_copy(c).start()

        @pl.when(c >= lag)
        def _():
            along_copy(c - lag).wait_recv()
            twin_copy(c - lag).start()

        return carry

    lax.fori_loop(0, chunks, turn, 0)

    def tail(i):
        along_copy(chunks - lag + i).wait_recv()
        twin_copy(chunks - lag + i).start()

    every(lag, tail)
    own_copy().wait_recv()
    every(chunks, lambda c: twin_copy(c).wait_recv())

    factor = math.exp(-CUTOFF) / (8.0 * (CUTOFF * LOG2E) ** 2)

    def multiply(g):
        acc = jnp.zeros((BS, rank), F32)
        for n in range(0, slots, 2):
            parts = jnp.concatenate([wide_ref[cols[g, n]], wide_ref[cols[g, n + 1]]], axis=0)
            acc = acc + jnp.dot(
                block_ref[g, :, n * BS : (n + 2) * BS], parts, preferred_element_type=F32
            )
        image = acc * factor + NUGGET * own_ref[g].astype(F32)
        image_ref[g] = image
        high = image.astype(BF16)
        low = (image - high.astype(F32)).astype(BF16)
        pair = jnp.concatenate([high, low], axis=1)
        local_ref[...] += lax.dot_general(
            high, pair, (((0,), (0,)), ((), ())), preferred_element_type=F32
        )

    every(rows, multiply)
    cross = local_ref[:, rank:]
    part = local_ref[:, :rank] + cross + jnp.transpose(cross)
    part_ref[...] = part.reshape(part_ref.shape)

    def copy1(k):
        p, dev = peer_q(k)
        return remote(part_ref.at[p], got1.at[q], s1.at[k], r1.at[k], dev)

    def copy2(k):
        return remote(mine, got2.at[r], s2.at[k], r2.at[k], peer_r(k)[1])

    def copy3(k):
        return remote(whole, got3.at[q], s3.at[k], r3.at[k], peer_q(k)[1])

    def others(do):
        def step(k, c):
            do(k)
            return c

        lax.fori_loop(1, 16, step, 0)

    others(lambda k: copy1(k).start())
    got1[q] = part_ref[q]
    others(lambda k: copy1(k).wait_recv())
    mine[...] = jnp.sum(got1[...], axis=0)
    others(lambda k: copy2(k).start())
    got2[r] = mine[...]
    others(lambda k: copy2(k).wait_recv())
    whole[...] = jnp.sum(got2[...], axis=0) * (1.0 / total)
    others(lambda k: copy3(k).start())
    got3[q] = whole[...]
    others(lambda k: copy3(k).wait_recv())
    gram_ref[...] = got3[...]

    for i in range(4):
        place_copy(i).wait_send()
    own_copy().wait_send()
    every(chunks, lambda c: cross_copy(c).wait_send())
    every(chunks, lambda c: along_copy(c).wait_send())
    every(chunks, lambda c: twin_copy(c).wait_send())
    others(lambda k: copy1(k).wait_send())
    others(lambda k: copy2(k).wait_send())
    others(lambda k: copy3(k).wait_send())


def image_and_gram(cols, scale, mine, own, total):
    rows, size, rank = own.shape
    slots = cols.shape[1]
    chunks = 16
    vmem = pl.BlockSpec(memory_space=pltpu.VMEM)
    smem = pl.BlockSpec(memory_space=pltpu.SMEM)
    dma = pltpu.SemaphoreType.DMA
    piece = rank // 16
    image, gram = pl.pallas_call(
        functools.partial(image_kernel, total),
        name="image",
        out_shape=(
            jax.ShapeDtypeStruct((rows, size, rank), F32),
            jax.ShapeDtypeStruct((16, piece, rank), F32),
        ),
        in_specs=[smem, smem, vmem, vmem],
        out_specs=(vmem, vmem),
        scratch_shapes=[
            pltpu.VMEM((rows, size, slots * size), BF16),
            pltpu.VMEM((STEPS * rows, size, rank), BF16),
            pltpu.VMEM((STEPS, rows * 4, size), BF16),
            pltpu.VMEM((STEPS * rows, 16, size), BF16),
            pltpu.VMEM((rows, 32, size), F32),
            pltpu.VMEM((rank, 2 * rank), F32),
        ]
        + [pltpu.VMEM((16, piece, rank), F32)] * 4
        + [pltpu.VMEM((piece, rank), F32)] * 2
        + [dma((4,))] * 2
        + [dma((chunks,))] * 6
        + [dma(())] * 2
        + [dma((16,))] * 6,
        compiler_params=pltpu.CompilerParams(
            collective_id=1, has_side_effects=True, vmem_limit_bytes=58 << 20
        ),
    )(cols, scale, mine, own)
    return image, gram.reshape(rank, rank)


def nt(a, b):
    return lax.dot_general(
        a, b, (((1,), (1,)), ((), ())), precision=HIGHEST, preferred_element_type=F32
    )


def nn(a, b):
    return jnp.dot(a, b, precision=HIGHEST, preferred_element_type=F32)


def basis_kernel(gram_ref, image_ref, basis_ref, factor_ref, inverse_ref, work_ref):
    n = gram_ref.shape[0]

    @pl.when(pl.program_id(0) == 0)
    def _():
        row = lax.broadcasted_iota(jnp.int32, (n, n), 0)
        col = lax.broadcasted_iota(jnp.int32, (n, n), 1)
        diag = row == col
        weight = jnp.where(row > col, 1.0, jnp.where(diag, 0.5, 0.0)).astype(F32)
        eye = jnp.where(diag, 1.0, 0.0).astype(F32)
        gram = gram_ref[...]
        only = jnp.where(diag, gram, 0.0)
        down = lax.rsqrt(jnp.sum(only, axis=1, keepdims=True))
        across = lax.rsqrt(jnp.sum(only, axis=0, keepdims=True))
        first = gram * down * across - eye
        inverse_ref[...] = (eye - first * weight) * across

        def unsettled(state):
            size, turn = state
            return jnp.logical_and(jnp.logical_not(size < 1e-6), turn < 8)

        def refine(state):
            turn = state[1]
            x = inverse_ref[...]
            gap = nt(nn(x, gram_ref[...]), x) - eye
            inverse_ref[...] = x - nn(gap * weight, x)
            return jnp.sum(gap * gap), turn + 1

        size, _ = lax.while_loop(unsettled, refine, (jnp.sum(first * first), jnp.int32(0)))
        settled = size < 1e-6

        @pl.when(settled)
        def _():
            factor_ref[...] = jnp.where(row <= col, nn(inverse_ref[...], gram_ref[...]), 0.0)

        @pl.when(jnp.logical_not(settled))
        def _():
            work_ref[:, :n] = gram_ref[...]
            work_ref[:, n:] = eye
            wide = lax.broadcasted_iota(jnp.int32, (n, 2 * n), 1)
            tall = lax.broadcasted_iota(jnp.int32, (n, 1), 0)

            def eliminate(k, c):
                m = work_ref[...]
                pivot_row = jnp.sum(jnp.where(tall == k, m, 0.0), axis=0, keepdims=True)
                column = jnp.sum(jnp.where(wide == k, m, 0.0), axis=1, keepdims=True)
                pivot = jnp.sum(jnp.where(tall == k, column, 0.0), axis=0, keepdims=True)
                ratio = jnp.where(tall > k, column / pivot, 0.0)
                work_ref[...] = m - ratio * pivot_row
                return c

            lax.fori_loop(0, n, eliminate, 0)
            upper = work_ref[:, :n]
            scale = lax.rsqrt(jnp.sum(jnp.where(diag, upper, 0.0), axis=1, keepdims=True))
            factor_ref[...] = jnp.where(row <= col, upper * scale, 0.0)
            inverse_ref[...] = work_ref[:, n:] * scale

    x = inverse_ref[...]
    xh = x.astype(BF16)
    xl = (x - xh.astype(F32)).astype(BF16)
    image = image_ref[...]
    high = image.astype(BF16)
    low = (image - high.astype(F32)).astype(BF16)

    def times(a, b):
        return lax.dot_general(a, b, (((1,), (1,)), ((), ())), preferred_element_type=F32)

    basis_ref[...] = times(high, xh) + times(high, xl) + times(low, xh)


def basis_and_factor(gram, image):
    n = gram.shape[0]
    rows = image.shape[0]
    step = 512
    return pl.pallas_call(
        basis_kernel,
        name="basis",
        grid=(rows // step,),
        out_shape=(
            jax.ShapeDtypeStruct((rows, n), F32),
            jax.ShapeDtypeStruct((n, n), F32),
        ),
        in_specs=[
            pl.BlockSpec((n, n), lambda i: (0, 0)),
            pl.BlockSpec((step, n), lambda i: (i, 0)),
        ],
        out_specs=(
            pl.BlockSpec((step, n), lambda i: (i, 0)),
            pl.BlockSpec((n, n), lambda i: (0, 0)),
        ),
        scratch_shapes=[pltpu.VMEM((n, n), F32), pltpu.VMEM((n, 2 * n), F32)],
    )(gram, image)


def on_device(panel, coords, neighbours, ranges):
    block_count = neighbours.shape[0]
    block_size = panel.shape[0] // block_count
    width = panel.shape[1]
    sector_count = lax.axis_size("sector")
    slab_count = lax.axis_size("depth")
    my_sector = lax.axis_index("sector")
    my_slab = lax.axis_index("depth")
    blocked = panel.reshape(block_count, block_size, width)

    low = jnp.stack([my_sector * AZ_SEC, 32, my_slab * DZ + DZ // 2]).astype(jnp.int32)
    inside = (coords - low[:, None]).reshape(3, block_count, block_size)
    inside = jnp.concatenate([inside, jnp.ones_like(inside[:1])], axis=0)
    mine = jnp.transpose(inside, (1, 0, 2)).reshape(4 * block_count, block_size).astype(BF16)
    scale = (LOG2E / ranges) ** 2

    column_sector = neighbours // (slab_count * block_count)
    step_away = (column_sector - my_sector + 2) % sector_count
    local_column = step_away * block_count + neighbours % block_count

    total_cells = float(panel.shape[0] * sector_count * slab_count)
    image, gram = image_and_gram(local_column, scale, mine, blocked, total_cells)
    image = image.reshape(block_count * block_size, width)
    basis, factor = basis_and_factor(gram, image)
    return (basis, factor)


def solution(mesh):
    in_specs = (
        P(("sector", "depth"), None),
        P(None, ("sector", "depth")),
        P(("sector", "depth"), None),
        P(),
    )
    out_specs = (P(("sector", "depth"), None), P())
    return jax.shard_map(
        on_device, mesh=mesh, in_specs=in_specs, out_specs=out_specs, check_vma=False
    )
```

```python
import functools
import math

import jax
import jax.numpy as jnp
from jax import lax
from jax.experimental import pallas as pl
from jax.experimental.pallas import tpu as pltpu
from jax.sharding import PartitionSpec as P

AZ_SEC = 8
DZ = 8
CUTOFF = 3.0
NUGGET = 0.5
BS = 128
LOG2E = 1.4426950408889634
MESH = pl.DeviceIdType.MESH
F32 = jnp.float32
BF16 = jnp.bfloat16
HIGHEST = lax.Precision.HIGHEST


STEPS = 5


def place():
    s = lax.axis_index("sector")
    d = lax.axis_index("depth")
    return s // 4, (s // 2) % 2, s % 2, d // 8, d % 8


def short(value):
    return value.astype(BF16).astype(F32)


def pieces(value):
    one = short(value)
    two = short(value - one)
    return one, two, value - one - two


def image_kernel(
    total, slabs, near, ranges, coords_ref, own_ref, image_ref, gram_ref,
    block_ref, wide_ref, place_ref, mine_ref, point_ref, right_ref, left_ref, local_ref,
    part_ref, got1, got2, got3, got4, one_sum, two_sum, three_sum,
    place_s, place_r, cross_s, cross_r, along_s, along_r, twin_s, twin_r, own_s, own_r,
    s1, r1, s2, r2, s3, r3, s4, r4,
):
    rows, rank = own_ref.shape[0], own_ref.shape[2]
    slots = near.shape[1]
    chunks = cross_s.shape[0]
    size = rows // chunks
    y, xh, core, xl, z = place()
    s = lax.axis_index("sector")
    d = lax.axis_index("depth")
    x = xh * 2 + xl
    a = core * 4 + x

    def sector(k):
        return lax.rem(s + k + 16, 16), d

    def peer_a(k):
        p = lax.rem(a + k, 8)
        px = lax.rem(p, 4)
        return p, (y * 4 + (px // 2) * 2 + p // 4, lax.rem(px, 2) * 8 + z)

    def peer_y(k):
        return lax.rem(s + 4 * k, 16), d

    def peer_z(k):
        return s, xl * 8 + lax.rem(z + k, 8)

    barrier = pltpu.get_barrier_semaphore()
    greeted = [sector(k) for k in (-2, -1, 1, 2)]
    greeted += [peer_y(k) for k in range(1, 4)]
    greeted += [peer_a(k)[1] for k in range(1, 8)] + [peer_z(k) for k in range(1, 8)]
    for device in greeted:
        pl.semaphore_signal(barrier, inc=1, device_id=device, device_id_type=MESH)

    corner = lax.broadcasted_iota(jnp.int32, (3, 1), 0)
    corner = jnp.where(corner == 0, s * AZ_SEC, jnp.where(corner == 1, 32, d * DZ + DZ // 2))
    point_ref[...] = jnp.ones_like(point_ref)
    for g in range(rows):
        inside = coords_ref[:, g * BS : (g + 1) * BS] - corner
        point_ref[4 * g : 4 * g + 3, :] = inside.astype(F32)
    mine_ref[...] = point_ref[...].astype(BF16)

    shift = (slabs * rows).bit_length() - 1

    def column(g, n):
        block = near[g, n]
        step = lax.rem(lax.shift_right_logical(block, shift) - s + 18, 16)
        return jnp.minimum(step, STEPS - 1) * rows + lax.rem(block, rows)

    pl.semaphore_wait(barrier, len(greeted))

    opposite = sector(2 - 4 * xh)
    onward = sector(4 - 8 * xh)
    across_at = (4 - 4 * xh) * rows
    along_at = 4 * xh * rows
    twin = sector(1 - 2 * core)
    twin_from = (4 - 4 * core) * rows
    twin_to = (3 - 2 * core) * rows
    own_to = (1 + 2 * core) * rows

    def remote(src, dst, send, recv, dev):
        return pltpu.make_async_remote_copy(
            src, dst, send, recv, device_id=dev, device_id_type=MESH
        )

    def place_copy(i):
        k = (-2, -1, 1, 2)[i]
        return remote(mine_ref, place_ref.at[2 - k], place_s.at[i], place_r.at[i], sector(k))

    def cross_copy(c):
        return remote(
            own_ref.at[pl.ds(c * size, size)],
            wide_ref.at[pl.ds(4 * xh * rows + c * size, size)],
            cross_s.at[c], cross_r.at[c], opposite,
        )

    def along_copy(c):
        return remote(
            wide_ref.at[pl.ds(across_at + c * size, size)],
            wide_ref.at[pl.ds(along_at + c * size, size)],
            along_s.at[c], along_r.at[c], onward,
        )

    def twin_copy(c):
        return remote(
            wide_ref.at[pl.ds(twin_from + c * size, size)],
            wide_ref.at[pl.ds(twin_to + c * size, size)],
            twin_s.at[c], twin_r.at[c], twin,
        )

    def own_copy():
        return remote(own_ref, wide_ref.at[pl.ds(own_to, rows)], own_s, own_r, twin)

    def every(count, do):
        def step(k, c):
            do(k)
            return c

        lax.fori_loop(0, count, step, 0)

    for i in range(4):
        place_copy(i).start()
    window = 4
    every(window, lambda c: cross_copy(c).start())
    own_copy().start()
    wide_ref[pl.ds(2 * rows, rows)] = own_ref[...]
    local_ref[...] = jnp.zeros_like(local_ref)

    line = lax.broadcasted_iota(jnp.int32, (1, 8, BS), 1)
    w = jnp.where(line == 0, ranges[0], jnp.where(line == 1, ranges[1], ranges[2]))
    w = LOG2E / w
    w = jnp.where(line < 3, w * w, 0.0)

    def spread(ref_value, step):
        even = ref_value.astype(F32).reshape(rows // 2, 8, BS)
        odd = jnp.concatenate([even[:, 4:], even[:, :4]], axis=1)
        both = jnp.stack([even, odd], axis=1).reshape(rows, 8, BS)
        both = both + jnp.where(line == 0, 8.0 * (step - 2) - 4.0, 0.0)
        norm = jnp.sum(both * both * w, axis=1, keepdims=True)
        return both, norm

    def put_right(both, norm, step):
        n1, n2, n3 = pieces(norm)
        tail = jnp.where(line == 4, n1, jnp.where(line == 5, n2, jnp.where(line == 6, n3, 0.0)))
        base = jnp.where(line < 4, both, tail)
        twice = jnp.concatenate([base, base], axis=1).astype(BF16)
        right_ref[pl.ds(step * rows, rows)] = twice

    both, norm = spread(point_ref[...], 2)
    put_right(both, norm, 2)
    full = jnp.where(line < 3, -2.0 * w * both, jnp.where(line == 3, norm, 0.0))
    a1, a2, a3 = pieces(full)
    a1 = a1 + jnp.where(jnp.logical_and(line > 3, line < 7), 1.0, 0.0)
    left_ref[...] = jnp.concatenate([a1, a2, a3, jnp.zeros_like(a1)], axis=1)
    for i in range(4):
        place_copy(i).wait_recv()
    for step in (0, 1, 3, 4):
        both, norm = spread(place_ref[step], step)
        put_right(both, norm, step)

    def build(g):
        left = jnp.transpose(left_ref[g]).astype(BF16)
        for n in range(0, slots, 2):
            right = jnp.concatenate([right_ref[column(g, n)], right_ref[column(g, n + 1)]], axis=1)
            right = jnp.concatenate([right, right], axis=0)
            square = jnp.dot(left, right, preferred_element_type=F32)
            square = jnp.maximum(square, 1e-10)
            rest = CUTOFF * LOG2E - square * lax.rsqrt(square)
            taper = jnp.maximum(rest, 0.0)
            block = jnp.exp2(rest) * taper * taper
            block_ref[g, :, n * BS : (n + 2) * BS] = block.astype(BF16)

    lag = 2

    def turn(c, carry):
        every(size, lambda i: build(c * size + i))
        cross_copy(c).wait_recv()
        along_copy(c).start()

        @pl.when(c + window < chunks)
        def _():
            cross_copy(c + window).start()

        @pl.when(c >= lag)
        def _():
            along_copy(c - lag).wait_recv()
            twin_copy(c - lag).start()

        return carry

    lax.fori_loop(0, chunks, turn, 0)

    def tail(i):
        along_copy(chunks - lag + i).wait_recv()
        twin_copy(chunks - lag + i).start()

    every(lag, tail)
    own_copy().wait_recv()
    every(chunks, lambda c: twin_copy(c).wait_recv())

    factor = math.exp(-CUTOFF) / (8.0 * (CUTOFF * LOG2E) ** 2)

    def multiply(g):
        acc = jnp.zeros((BS, rank), F32)
        for n in range(0, slots, 2):
            parts = jnp.concatenate([wide_ref[column(g, n)], wide_ref[column(g, n + 1)]], axis=0)
            acc = acc + jnp.dot(
                block_ref[g, :, n * BS : (n + 2) * BS], parts, preferred_element_type=F32
            )
        image = acc * factor + NUGGET * own_ref[g].astype(F32)
        image_ref[g] = image
        high = image.astype(BF16)
        low = (image - high.astype(F32)).astype(BF16)
        pair = jnp.concatenate([high, low], axis=1)
        local_ref[...] += lax.dot_general(
            high, pair, (((0,), (0,)), ((), ())), preferred_element_type=F32
        )

    every(rows, multiply)
    cross = local_ref[:, rank:]
    part = local_ref[:, :rank] + cross + jnp.transpose(cross)
    part_ref[...] = part.reshape(part_ref.shape)

    def copy1(k):
        p, device = peer_a(k)
        return remote(part_ref.at[p], got1.at[a], s1.at[k], r1.at[k], device)

    def copy2(k):
        return remote(one_sum, got2.at[y], s2.at[k], r2.at[k], peer_y(k))

    def copy3(k):
        return remote(two_sum, got3.at[z], s3.at[k], r3.at[k], peer_z(k))

    def copy4(k):
        return remote(three_sum, got4.at[a], s4.at[k], r4.at[k], peer_a(k)[1])

    def exchange(copy, count, own, value, got):
        for k in range(1, count):
            copy(k).start()
        got[own] = value
        for k in range(1, count):
            copy(k).wait_recv()

    exchange(copy1, 8, a, part_ref[a], got1)
    one_sum[...] = jnp.sum(got1[...], axis=0)
    exchange(copy2, 4, y, one_sum[...], got2)
    two_sum[...] = jnp.sum(got2[...], axis=0)
    exchange(copy3, 8, z, two_sum[...], got3)
    three_sum[...] = jnp.sum(got3[...], axis=0) * (1.0 / total)
    exchange(copy4, 8, a, three_sum[...], got4)
    gram_ref[...] = got4[...]

    for i in range(4):
        place_copy(i).wait_send()
    own_copy().wait_send()
    every(chunks, lambda c: cross_copy(c).wait_send())
    every(chunks, lambda c: along_copy(c).wait_send())
    every(chunks, lambda c: twin_copy(c).wait_send())
    for copy, count in ((copy1, 8), (copy2, 4), (copy3, 8), (copy4, 8)):
        for k in range(1, count):
            copy(k).wait_send()


def image_and_gram(near, ranges, coords, own, slabs, total):
    rows, size, rank = own.shape
    slots = near.shape[1]
    chunks = 16
    vmem = pl.BlockSpec(memory_space=pltpu.VMEM)
    smem = pl.BlockSpec(memory_space=pltpu.SMEM)
    dma = pltpu.SemaphoreType.DMA
    piece = rank // 8
    image, gram = pl.pallas_call(
        functools.partial(image_kernel, total, slabs),
        name="image",
        out_shape=(
            jax.ShapeDtypeStruct((rows, size, rank), F32),
            jax.ShapeDtypeStruct((8, piece, rank), F32),
        ),
        in_specs=[smem, smem, vmem, vmem],
        out_specs=(vmem, vmem),
        scratch_shapes=[
            pltpu.VMEM((rows, size, slots * size), BF16),
            pltpu.VMEM((STEPS * rows, size, rank), BF16),
            pltpu.VMEM((STEPS, rows * 4, size), BF16),
            pltpu.VMEM((rows * 4, size), BF16),
            pltpu.VMEM((rows * 4, size), F32),
            pltpu.VMEM((STEPS * rows, 16, size), BF16),
            pltpu.VMEM((rows, 32, size), F32),
            pltpu.VMEM((rank, 2 * rank), F32),
        ]
        + [pltpu.VMEM((n, piece, rank), F32) for n in (8, 8, 4, 8, 8)]
        + [pltpu.VMEM((piece, rank), F32)] * 3
        + [dma((4,))] * 2
        + [dma((chunks,))] * 6
        + [dma(())] * 2
        + [dma((n,)) for n in (8, 8, 4, 4, 8, 8, 8, 8)],
        compiler_params=pltpu.CompilerParams(
            collective_id=1, has_side_effects=True, vmem_limit_bytes=58 << 20
        ),
    )(near, ranges, coords, own)
    return image, gram.reshape(rank, rank)


def nt(a, b):
    return lax.dot_general(
        a, b, (((1,), (1,)), ((), ())), precision=HIGHEST, preferred_element_type=F32
    )


def nn(a, b):
    return jnp.dot(a, b, precision=HIGHEST, preferred_element_type=F32)


def basis_kernel(
    gram_ref, image_hbm, basis_hbm, factor_ref, inverse_ref, work_ref, image_ref, out_ref,
    in_sem, out_sem,
):
    n = gram_ref.shape[0]
    chunks = out_sem.shape[0]
    size = image_ref.shape[0] // chunks
    fetch = pltpu.make_async_copy(image_hbm, image_ref, in_sem)
    fetch.start()

    row = lax.broadcasted_iota(jnp.int32, (n, n), 0)
    col = lax.broadcasted_iota(jnp.int32, (n, n), 1)
    diag = row == col
    weight = jnp.where(row > col, 1.0, jnp.where(diag, 0.5, 0.0)).astype(F32)
    eye = jnp.where(diag, 1.0, 0.0).astype(F32)
    gram = gram_ref[...]
    only = jnp.where(diag, gram, 0.0)
    down = lax.rsqrt(jnp.sum(only, axis=1, keepdims=True))
    across = lax.rsqrt(jnp.sum(only, axis=0, keepdims=True))
    first = gram * down * across - eye
    inverse_ref[...] = (eye - first * weight) * across

    def unsettled(state):
        size, turn = state
        return jnp.logical_and(jnp.logical_not(size < 1e-6), turn < 8)

    def refine(state):
        turn = state[1]
        x = inverse_ref[...]
        gap = nt(nn(x, gram_ref[...]), x) - eye
        inverse_ref[...] = x - nn(gap * weight, x)
        return jnp.sum(gap * gap), turn + 1

    far, _ = lax.while_loop(unsettled, refine, (jnp.sum(first * first), jnp.int32(0)))
    settled = far < 1e-6

    @pl.when(settled)
    def _():
        factor_ref[...] = jnp.where(row <= col, nn(inverse_ref[...], gram_ref[...]), 0.0)

    @pl.when(jnp.logical_not(settled))
    def _():
        work_ref[:, :n] = gram_ref[...]
        work_ref[:, n:] = eye
        wide = lax.broadcasted_iota(jnp.int32, (n, 2 * n), 1)
        tall = lax.broadcasted_iota(jnp.int32, (n, 1), 0)

        def eliminate(k, c):
            m = work_ref[...]
            pivot_row = jnp.sum(jnp.where(tall == k, m, 0.0), axis=0, keepdims=True)
            column = jnp.sum(jnp.where(wide == k, m, 0.0), axis=1, keepdims=True)
            pivot = jnp.sum(jnp.where(tall == k, column, 0.0), axis=0, keepdims=True)
            ratio = jnp.where(tall > k, column / pivot, 0.0)
            work_ref[...] = m - ratio * pivot_row
            return c

        lax.fori_loop(0, n, eliminate, 0)
        upper = work_ref[:, :n]
        scale = lax.rsqrt(jnp.sum(jnp.where(diag, upper, 0.0), axis=1, keepdims=True))
        factor_ref[...] = jnp.where(row <= col, upper * scale, 0.0)
        inverse_ref[...] = work_ref[:, n:] * scale

    x = jnp.transpose(inverse_ref[...])
    xh = x.astype(BF16)
    xl = (x - xh.astype(F32)).astype(BF16)
    right = jnp.concatenate(
        [
            jnp.concatenate([xh, xl], axis=1),
            jnp.concatenate([xh, jnp.zeros_like(xl)], axis=1),
        ],
        axis=0,
    )
    fetch.wait()

    def send(i):
        piece = pl.ds(i * size, size)
        return pltpu.make_async_copy(out_ref.at[piece], basis_hbm.at[piece], out_sem.at[i])

    for i in range(chunks):
        image = image_ref[i * size : (i + 1) * size]
        high = image.astype(BF16)
        low = (image - high.astype(F32)).astype(BF16)
        both = jnp.concatenate([high, low], axis=1)
        product = jnp.dot(both, right, preferred_element_type=F32)
        out_ref[i * size : (i + 1) * size] = product[:, :n] + product[:, n:]
        send(i).start()
    for i in range(chunks):
        send(i).wait()


def basis_and_factor(gram, image):
    n = gram.shape[0]
    rows = image.shape[0]
    chunks = 8
    vmem = pl.BlockSpec(memory_space=pltpu.VMEM)
    hbm = pl.BlockSpec(memory_space=pl.ANY)
    return pl.pallas_call(
        basis_kernel,
        name="basis",
        out_shape=(
            jax.ShapeDtypeStruct((rows, n), F32),
            jax.ShapeDtypeStruct((n, n), F32),
        ),
        in_specs=[vmem, hbm],
        out_specs=(hbm, vmem),
        scratch_shapes=[
            pltpu.VMEM((n, n), F32),
            pltpu.VMEM((n, 2 * n), F32),
            pltpu.VMEM((rows, n), F32),
            pltpu.VMEM((rows, n), F32),
            pltpu.SemaphoreType.DMA(()),
            pltpu.SemaphoreType.DMA((chunks,)),
        ],
    )(gram, image)


def on_device(panel, coords, neighbours, ranges):
    block_count = neighbours.shape[0]
    block_size = panel.shape[0] // block_count
    width = panel.shape[1]
    sector_count = lax.axis_size("sector")
    slab_count = lax.axis_size("depth")
    blocked = panel.reshape(block_count, block_size, width)

    total_cells = float(panel.shape[0] * sector_count * slab_count)
    image, gram = image_and_gram(
        neighbours, ranges, coords, blocked, slab_count, total_cells
    )
    image = image.reshape(block_count * block_size, width)
    basis, factor = basis_and_factor(gram, image)
    return (basis, factor)


def solution(mesh):
    in_specs = (
        P(("sector", "depth"), None),
        P(None, ("sector", "depth")),
        P(("sector", "depth"), None),
        P(),
    )
    out_specs = (P(("sector", "depth"), None), P())
    return jax.shard_map(
        on_device, mesh=mesh, in_specs=in_specs, out_specs=out_specs, check_vma=False
    )
```

```python
import functools
import math

import jax
import jax.numpy as jnp
from jax import lax
from jax.experimental import pallas as pl
from jax.experimental.pallas import tpu as pltpu
from jax.sharding import PartitionSpec as P

AZ_SEC = 8
DZ = 8
CUTOFF = 3.0
NUGGET = 0.5
BS = 128
LOG2E = 1.4426950408889634
MESH = pl.DeviceIdType.MESH
F32 = jnp.float32
BF16 = jnp.bfloat16
HIGHEST = lax.Precision.HIGHEST


STEPS = 5


def place():
    s = lax.axis_index("sector")
    d = lax.axis_index("depth")
    return s // 4, (s // 2) % 2, s % 2, d // 8, d % 8


def short(value):
    return value.astype(BF16).astype(F32)


def pieces(value):
    one = short(value)
    two = short(value - one)
    return one, two, value - one - two


def image_kernel(
    total, slabs, near, ranges, coords_ref, own_ref, image_hbm, gram_ref,
    early_ref, late_ref, image_ref, wide_ref, place_ref, mine_ref, point_ref, right_ref, left_ref, local_ref,
    part_ref, got1, got2, got3, got4, one_sum, two_sum, three_sum,
    place_s, place_r, cross_s, cross_r, along_s, along_r, twin_s, twin_r, own_s, own_r,
    s1, r1, s2, r2, s3, r3, s4, r4, out_sem,
):
    rows, rank = own_ref.shape[0], own_ref.shape[2]
    slots = near.shape[1]
    chunks = cross_s.shape[0]
    size = rows // chunks
    y, xh, core, xl, z = place()
    s = lax.axis_index("sector")
    d = lax.axis_index("depth")
    x = xh * 2 + xl
    a = core * 4 + x

    def sector(k):
        return lax.rem(s + k + 16, 16), d

    def peer_a(k):
        p = lax.rem(a + k, 8)
        px = lax.rem(p, 4)
        return p, (y * 4 + (px // 2) * 2 + p // 4, lax.rem(px, 2) * 8 + z)

    def peer_y(k):
        return lax.rem(s + 4 * k, 16), d

    def peer_z(k):
        return s, xl * 8 + lax.rem(z + k, 8)

    barrier = pltpu.get_barrier_semaphore()
    greeted = [sector(k) for k in (-2, -1, 1, 2)]
    greeted += [peer_y(k) for k in range(1, 4)]
    greeted += [peer_a(k)[1] for k in range(1, 8)] + [peer_z(k) for k in range(1, 8)]
    for device in greeted:
        pl.semaphore_signal(barrier, inc=1, device_id=device, device_id_type=MESH)

    corner = lax.broadcasted_iota(jnp.int32, (3, 1), 0)
    corner = jnp.where(corner == 0, s * AZ_SEC, jnp.where(corner == 1, 32, d * DZ + DZ // 2))
    point_ref[...] = jnp.ones_like(point_ref)
    for g in range(rows):
        inside = coords_ref[:, g * BS : (g + 1) * BS] - corner
        point_ref[4 * g : 4 * g + 3, :] = inside.astype(F32)
    mine_ref[...] = point_ref[...].astype(BF16)

    shift = (slabs * rows).bit_length() - 1

    def column(g, n):
        block = near[g, n]
        step = lax.rem(lax.shift_right_logical(block, shift) - s + 18, 16)
        return jnp.minimum(step, STEPS - 1) * rows + lax.rem(block, rows)

    pl.semaphore_wait(barrier, len(greeted))

    opposite = sector(2 - 4 * xh)
    onward = sector(4 - 8 * xh)
    across_at = (4 - 4 * xh) * rows
    along_at = 4 * xh * rows
    twin = sector(1 - 2 * core)
    twin_from = (4 - 4 * core) * rows
    twin_to = (3 - 2 * core) * rows
    own_to = (1 + 2 * core) * rows

    def remote(src, dst, send, recv, dev):
        return pltpu.make_async_remote_copy(
            src, dst, send, recv, device_id=dev, device_id_type=MESH
        )

    def place_copy(i):
        k = (-2, -1, 1, 2)[i]
        return remote(mine_ref, place_ref.at[2 - k], place_s.at[i], place_r.at[i], sector(k))

    def cross_copy(c):
        return remote(
            own_ref.at[pl.ds(c * size, size)],
            wide_ref.at[pl.ds(4 * xh * rows + c * size, size)],
            cross_s.at[c], cross_r.at[c], opposite,
        )

    def along_copy(c):
        return remote(
            wide_ref.at[pl.ds(across_at + c * size, size)],
            wide_ref.at[pl.ds(along_at + c * size, size)],
            along_s.at[c], along_r.at[c], onward,
        )

    def twin_copy(c):
        return remote(
            wide_ref.at[pl.ds(twin_from + c * size, size)],
            wide_ref.at[pl.ds(twin_to + c * size, size)],
            twin_s.at[c], twin_r.at[c], twin,
        )

    def own_copy():
        return remote(own_ref, wide_ref.at[pl.ds(own_to, rows)], own_s, own_r, twin)

    def every(count, do):
        def step(k, c):
            do(k)
            return c

        lax.fori_loop(0, count, step, 0)

    for i in range(4):
        place_copy(i).start()
    window = 4
    cross_copy(0).start()
    wide_ref[pl.ds(2 * rows, rows)] = own_ref[...]
    local_ref[...] = jnp.zeros_like(local_ref)

    line = lax.broadcasted_iota(jnp.int32, (1, 8, BS), 1)
    w = jnp.where(line == 0, ranges[0], jnp.where(line == 1, ranges[1], ranges[2]))
    w = LOG2E / w
    w = jnp.where(line < 3, w * w, 0.0)

    def spread(ref_value, step):
        even = ref_value.astype(F32).reshape(rows // 2, 8, BS)
        odd = jnp.concatenate([even[:, 4:], even[:, :4]], axis=1)
        both = jnp.stack([even, odd], axis=1).reshape(rows, 8, BS)
        both = both + jnp.where(line == 0, 8.0 * (step - 2) - 4.0, 0.0)
        norm = jnp.sum(both * both * w, axis=1, keepdims=True)
        return both, norm

    def put_right(both, norm, step):
        n1, n2, n3 = pieces(norm)
        tail = jnp.where(line == 4, n1, jnp.where(line == 5, n2, jnp.where(line == 6, n3, 0.0)))
        base = jnp.where(line < 4, both, tail)
        twice = jnp.concatenate([base, base], axis=1).astype(BF16)
        right_ref[pl.ds(step * rows, rows)] = twice

    both, norm = spread(point_ref[...], 2)
    put_right(both, norm, 2)
    full = jnp.where(line < 3, -2.0 * w * both, jnp.where(line == 3, norm, 0.0))
    a1, a2, a3 = pieces(full)
    a1 = a1 + jnp.where(jnp.logical_and(line > 3, line < 7), 1.0, 0.0)
    left_ref[...] = jnp.concatenate([a1, a2, a3, jnp.zeros_like(a1)], axis=1)
    for i in range(4):
        place_copy(i).wait_recv()
    for c in range(1, window):
        cross_copy(c).start()
    own_copy().start()
    for step in (0, 1, 3, 4):
        both, norm = spread(place_ref[step], step)
        put_right(both, norm, step)

    def left_of(g):
        return jnp.transpose(left_ref[g]).astype(BF16)

    def block_pair(left, g, n):
        right = jnp.concatenate([right_ref[column(g, n)], right_ref[column(g, n + 1)]], axis=1)
        right = jnp.concatenate([right, right], axis=0)
        square = jnp.dot(left, right, preferred_element_type=F32)
        square = jnp.maximum(square, 1e-10)
        rest = CUTOFF * LOG2E - square * lax.rsqrt(square)
        taper = jnp.maximum(rest, 0.0)
        return (jnp.exp2(rest) * taper * taper).astype(BF16)

    def build(g):
        left = left_of(g)
        for n in range(0, slots, 2):
            early_ref[g, :, n * BS : (n + 2) * BS] = block_pair(left, g, n)

    early = early_ref.shape[0]
    late = late_ref.shape[0]
    share = early // late
    paced = early - 2
    lag = 2

    def turn(c, carry):
        def row(g, carry):
            build(g)
            return carry

        lax.fori_loop((c * paced) // chunks, ((c + 1) * paced) // chunks, row, 0)
        cross_copy(c).wait_recv()
        along_copy(c).start()

        @pl.when(c + window < chunks)
        def _():
            cross_copy(c + window).start()

        @pl.when(c >= lag)
        def _():
            along_copy(c - lag).wait_recv()
            twin_copy(c - lag).start()

        return carry

    lax.fori_loop(0, chunks, turn, 0)
    for g in range(paced, early):
        build(g)

    def tail(i):
        along_copy(chunks - lag + i).wait_recv()
        twin_copy(chunks - lag + i).start()

    every(lag, tail)
    own_copy().wait_recv()
    every(chunks, lambda c: twin_copy(c).wait_recv())

    factor = math.exp(-CUTOFF) / (8.0 * (CUTOFF * LOG2E) ** 2)

    def out_copy(g):
        return pltpu.make_async_copy(image_ref.at[g], image_hbm.at[g], out_sem.at[g])

    def multiply(g, source, at, beside):
        acc = jnp.zeros((BS, rank), F32)
        for n in range(0, slots, 2):
            parts = jnp.concatenate([wide_ref[column(g, n)], wide_ref[column(g, n + 1)]], axis=0)
            beside()
            acc = acc + jnp.dot(
                source[at, :, n * BS : (n + 2) * BS], parts, preferred_element_type=F32
            )
        image = acc * factor + NUGGET * own_ref[g].astype(F32)
        image_ref[g] = image
        out_copy(g).start()
        high = image.astype(BF16)
        low = (image - high.astype(F32)).astype(BF16)
        pair = jnp.concatenate([high, low], axis=1)
        local_ref[...] += lax.dot_general(
            high, pair, (((0,), (0,)), ((), ())), preferred_element_type=F32
        )

    def both_at_once(t):
        left = left_of(early + t)
        done = [0, 0]

        def beside():
            if done[0] % share == 0:
                n = 2 * done[1]
                late_ref[t, :, n * BS : (n + 2) * BS] = block_pair(left, early + t, n)
                done[1] += 1
            done[0] += 1

        for i in range(share):
            g = t * share + i
            multiply(g, early_ref, g, beside)

    every(late, both_at_once)
    every(late, lambda t: multiply(early + t, late_ref, t, lambda: None))
    cross = local_ref[:, rank:]
    part = local_ref[:, :rank] + cross + jnp.transpose(cross)
    part_ref[...] = part.reshape(part_ref.shape)

    def copy1(k):
        p, device = peer_a(k)
        return remote(part_ref.at[p], got1.at[a], s1.at[k], r1.at[k], device)

    def copy2(k):
        return remote(one_sum, got2.at[y], s2.at[k], r2.at[k], peer_y(k))

    def copy3(k):
        return remote(two_sum, got3.at[z], s3.at[k], r3.at[k], peer_z(k))

    def copy4(k):
        return remote(three_sum, got4.at[a], s4.at[k], r4.at[k], peer_a(k)[1])

    def exchange(copy, count, own, value, got):
        for k in range(1, count):
            copy(k).start()
        got[own] = value
        for k in range(1, count):
            copy(k).wait_recv()

    exchange(copy1, 8, a, part_ref[a], got1)
    one_sum[...] = jnp.sum(got1[...], axis=0)
    exchange(copy2, 4, y, one_sum[...], got2)
    two_sum[...] = jnp.sum(got2[...], axis=0)
    exchange(copy3, 8, z, two_sum[...], got3)
    three_sum[...] = jnp.sum(got3[...], axis=0) * (1.0 / total)
    exchange(copy4, 8, a, three_sum[...], got4)
    gram_ref[...] = got4[...]

    every(rows, lambda g: out_copy(g).wait())
    for i in range(4):
        place_copy(i).wait_send()
    own_copy().wait_send()
    every(chunks, lambda c: cross_copy(c).wait_send())
    every(chunks, lambda c: along_copy(c).wait_send())
    every(chunks, lambda c: twin_copy(c).wait_send())
    for copy, count in ((copy1, 8), (copy2, 4), (copy3, 8), (copy4, 8)):
        for k in range(1, count):
            copy(k).wait_send()


def image_and_gram(near, ranges, coords, own, slabs, total):
    rows, size, rank = own.shape
    slots = near.shape[1]
    chunks = 16
    late = rows // 8
    early = rows - late
    vmem = pl.BlockSpec(memory_space=pltpu.VMEM)
    smem = pl.BlockSpec(memory_space=pltpu.SMEM)
    dma = pltpu.SemaphoreType.DMA
    piece = rank // 8
    image, gram = pl.pallas_call(
        functools.partial(image_kernel, total, slabs),
        name="image",
        out_shape=(
            jax.ShapeDtypeStruct((rows, size, rank), F32),
            jax.ShapeDtypeStruct((8, piece, rank), F32),
        ),
        in_specs=[smem, smem, vmem, vmem],
        out_specs=(pl.BlockSpec(memory_space=pl.ANY), vmem),
        scratch_shapes=[
            pltpu.VMEM((early, size, slots * size), BF16),
            pltpu.VMEM((late, size, slots * size), BF16),
            pltpu.VMEM((rows, size, rank), F32),
            pltpu.VMEM((STEPS * rows, size, rank), BF16),
            pltpu.VMEM((STEPS, rows * 4, size), BF16),
            pltpu.VMEM((rows * 4, size), BF16),
            pltpu.VMEM((rows * 4, size), F32),
            pltpu.VMEM((STEPS * rows, 16, size), BF16),
            pltpu.VMEM((rows, 32, size), F32),
            pltpu.VMEM((rank, 2 * rank), F32),
        ]
        + [pltpu.VMEM((n, piece, rank), F32) for n in (8, 8, 4, 8, 8)]
        + [pltpu.VMEM((piece, rank), F32)] * 3
        + [dma((4,))] * 2
        + [dma((chunks,))] * 6
        + [dma(())] * 2
        + [dma((n,)) for n in (8, 8, 4, 4, 8, 8, 8, 8, rows)],
        compiler_params=pltpu.CompilerParams(
            collective_id=1, has_side_effects=True, vmem_limit_bytes=58 << 20
        ),
    )(near, ranges, coords, own)
    return image, gram.reshape(rank, rank)


def nt(a, b):
    return lax.dot_general(
        a, b, (((1,), (1,)), ((), ())), precision=HIGHEST, preferred_element_type=F32
    )


def nn(a, b):
    return jnp.dot(a, b, precision=HIGHEST, preferred_element_type=F32)


def basis_kernel(
    gram_ref, image_hbm, basis_hbm, factor_ref, inverse_ref, work_ref, image_ref, out_ref,
    in_sem, out_sem,
):
    n = gram_ref.shape[0]
    chunks = out_sem.shape[0]
    size = image_ref.shape[0] // chunks
    fetch = pltpu.make_async_copy(image_hbm, image_ref, in_sem)
    fetch.start()

    row = lax.broadcasted_iota(jnp.int32, (n, n), 0)
    col = lax.broadcasted_iota(jnp.int32, (n, n), 1)
    diag = row == col
    weight = jnp.where(row > col, 1.0, jnp.where(diag, 0.5, 0.0)).astype(F32)
    eye = jnp.where(diag, 1.0, 0.0).astype(F32)
    gram = gram_ref[...]
    only = jnp.where(diag, gram, 0.0)
    down = lax.rsqrt(jnp.sum(only, axis=1, keepdims=True))
    across = lax.rsqrt(jnp.sum(only, axis=0, keepdims=True))
    first = gram * down * across - eye
    inverse_ref[...] = (eye - first * weight) * across

    def unsettled(state):
        size, turn = state
        return jnp.logical_and(jnp.logical_not(size < 1e-6), turn < 8)

    def refine(state):
        turn = state[1]
        x = inverse_ref[...]
        gap = nt(nn(x, gram_ref[...]), x) - eye
        inverse_ref[...] = x - nn(gap * weight, x)
        return jnp.sum(gap * gap), turn + 1

    far, _ = lax.while_loop(unsettled, refine, (jnp.sum(first * first), jnp.int32(0)))
    settled = far < 1e-6

    @pl.when(settled)
    def _():
        factor_ref[...] = jnp.where(row <= col, nn(inverse_ref[...], gram_ref[...]), 0.0)

    @pl.when(jnp.logical_not(settled))
    def _():
        work_ref[:, :n] = gram_ref[...]
        work_ref[:, n:] = eye
        wide = lax.broadcasted_iota(jnp.int32, (n, 2 * n), 1)
        tall = lax.broadcasted_iota(jnp.int32, (n, 1), 0)

        def eliminate(k, c):
            m = work_ref[...]
            pivot_row = jnp.sum(jnp.where(tall == k, m, 0.0), axis=0, keepdims=True)
            column = jnp.sum(jnp.where(wide == k, m, 0.0), axis=1, keepdims=True)
            pivot = jnp.sum(jnp.where(tall == k, column, 0.0), axis=0, keepdims=True)
            ratio = jnp.where(tall > k, column / pivot, 0.0)
            work_ref[...] = m - ratio * pivot_row
            return c

        lax.fori_loop(0, n, eliminate, 0)
        upper = work_ref[:, :n]
        scale = lax.rsqrt(jnp.sum(jnp.where(diag, upper, 0.0), axis=1, keepdims=True))
        factor_ref[...] = jnp.where(row <= col, upper * scale, 0.0)
        inverse_ref[...] = work_ref[:, n:] * scale

    x = jnp.transpose(inverse_ref[...])
    xh = x.astype(BF16)
    xl = (x - xh.astype(F32)).astype(BF16)
    right = jnp.concatenate(
        [
            jnp.concatenate([xh, xl], axis=1),
            jnp.concatenate([xh, jnp.zeros_like(xl)], axis=1),
        ],
        axis=0,
    )
    fetch.wait()

    def send(i):
        piece = pl.ds(i * size, size)
        return pltpu.make_async_copy(out_ref.at[piece], basis_hbm.at[piece], out_sem.at[i])

    for i in range(chunks):
        image = image_ref[i * size : (i + 1) * size]
        high = image.astype(BF16)
        low = (image - high.astype(F32)).astype(BF16)
        both = jnp.concatenate([high, low], axis=1)
        product = jnp.dot(both, right, preferred_element_type=F32)
        out_ref[i * size : (i + 1) * size] = product[:, :n] + product[:, n:]
        send(i).start()
    for i in range(chunks):
        send(i).wait()


def basis_and_factor(gram, image):
    n = gram.shape[0]
    rows = image.shape[0]
    chunks = 8
    vmem = pl.BlockSpec(memory_space=pltpu.VMEM)
    hbm = pl.BlockSpec(memory_space=pl.ANY)
    return pl.pallas_call(
        basis_kernel,
        name="basis",
        out_shape=(
            jax.ShapeDtypeStruct((rows, n), F32),
            jax.ShapeDtypeStruct((n, n), F32),
        ),
        in_specs=[vmem, hbm],
        out_specs=(hbm, vmem),
        scratch_shapes=[
            pltpu.VMEM((n, n), F32),
            pltpu.VMEM((n, 2 * n), F32),
            pltpu.VMEM((rows, n), F32),
            pltpu.VMEM((rows, n), F32),
            pltpu.SemaphoreType.DMA(()),
            pltpu.SemaphoreType.DMA((chunks,)),
        ],
    )(gram, image)


def on_device(panel, coords, neighbours, ranges):
    block_count = neighbours.shape[0]
    block_size = panel.shape[0] // block_count
    width = panel.shape[1]
    sector_count = lax.axis_size("sector")
    slab_count = lax.axis_size("depth")
    blocked = panel.reshape(block_count, block_size, width)

    total_cells = float(panel.shape[0] * sector_count * slab_count)
    image, gram = image_and_gram(
        neighbours, ranges, coords, blocked, slab_count, total_cells
    )
    image = image.reshape(block_count * block_size, width)
    basis, factor = basis_and_factor(gram, image)
    return (basis, factor)


def solution(mesh):
    in_specs = (
        P(("sector", "depth"), None),
        P(None, ("sector", "depth")),
        P(("sector", "depth"), None),
        P(),
    )
    out_specs = (P(("sector", "depth"), None), P())
    return jax.shard_map(
        on_device, mesh=mesh, in_specs=in_specs, out_specs=out_specs, check_vma=False
    )
```

```python
import functools
import math

import jax
import jax.numpy as jnp
from jax import lax
from jax.experimental import pallas as pl
from jax.experimental.pallas import tpu as pltpu
from jax.sharding import PartitionSpec as P

AZ_SEC = 8
DZ = 8
CUTOFF = 3.0
NUGGET = 0.5
BS = 128
LOG2E = 1.4426950408889634
MESH = pl.DeviceIdType.MESH
F32 = jnp.float32
BF16 = jnp.bfloat16
HIGHEST = lax.Precision.HIGHEST


STEPS = 5


def place():
    s = lax.axis_index("sector")
    d = lax.axis_index("depth")
    return s // 4, (s // 2) % 2, s % 2, d // 8, d % 8


def short(value):
    return value.astype(BF16).astype(F32)


def pieces(value):
    one = short(value)
    two = short(value - one)
    return one, two, value - one - two


def image_kernel(
    total, slabs, near, ranges, coords_ref, own_ref, image_hbm, gram_ref,
    early_ref, late_ref, image_ref, wide_ref, place_ref, mine_ref, point_ref, right_ref, left_ref, local_ref,
    part_ref, got1, got2, got3, got4, one_sum, two_sum, three_sum,
    place_s, place_r, cross_s, cross_r, along_s, along_r, twin_s, twin_r, own_s, own_r,
    s1, r1, s2, r2, s3, r3, s4, r4, out_sem,
):
    rows, rank = own_ref.shape[0], own_ref.shape[2]
    slots = near.shape[1]
    chunks = cross_r.shape[0]
    size = rows // chunks
    y, xh, core, xl, z = place()
    s = lax.axis_index("sector")
    d = lax.axis_index("depth")
    x = xh * 2 + xl
    a = core * 4 + x

    def sector(k):
        return lax.rem(s + k + 16, 16), d

    def peer_a(k):
        p = lax.rem(a + k, 8)
        px = lax.rem(p, 4)
        return p, (y * 4 + (px // 2) * 2 + p // 4, lax.rem(px, 2) * 8 + z)

    def peer_y(k):
        return lax.rem(s + 4 * k, 16), d

    def peer_z(k):
        return s, xl * 8 + lax.rem(z + k, 8)

    barrier = pltpu.get_barrier_semaphore()
    greeted = [sector(k) for k in (-2, -1, 1, 2)]
    greeted += [peer_y(k) for k in range(1, 4)]
    greeted += [peer_a(k)[1] for k in range(1, 8)] + [peer_z(k) for k in range(1, 8)]
    for device in greeted:
        pl.semaphore_signal(barrier, inc=1, device_id=device, device_id_type=MESH)

    corner = lax.broadcasted_iota(jnp.int32, (3, 1), 0)
    corner = jnp.where(corner == 0, s * AZ_SEC, jnp.where(corner == 1, 32, d * DZ + DZ // 2))
    point_ref[...] = jnp.ones_like(point_ref)
    for g in range(rows):
        inside = coords_ref[:, g * BS : (g + 1) * BS] - corner
        point_ref[4 * g : 4 * g + 3, :] = inside.astype(F32)
    mine_ref[...] = point_ref[...].astype(BF16)

    shift = (slabs * rows).bit_length() - 1

    def column(g, n):
        block = near[g, n]
        step = lax.rem(lax.shift_right_logical(block, shift) - s + 18, 16)
        return jnp.minimum(step, STEPS - 1) * rows + lax.rem(block, rows)

    pl.semaphore_wait(barrier, len(greeted))

    opposite = sector(2 - 4 * xh)
    onward = sector(4 - 8 * xh)
    across_at = (4 - 4 * xh) * rows
    along_at = 4 * xh * rows
    twin = sector(1 - 2 * core)
    twin_from = (4 - 4 * core) * rows
    twin_to = (3 - 2 * core) * rows
    own_to = (1 + 2 * core) * rows

    def remote(src, dst, send, recv, dev):
        return pltpu.make_async_remote_copy(
            src, dst, send, recv, device_id=dev, device_id_type=MESH
        )

    def place_copy(i):
        k = (-2, -1, 1, 2)[i]
        return remote(mine_ref, place_ref.at[2 - k], place_s, place_r, sector(k))

    def all_places():
        four = place_ref.at[pl.ds(0, 4)]
        return remote(four, four, place_s, place_r, twin)

    def all_rows(send, recv):
        whole = wide_ref.at[pl.ds(0, rows)]
        return remote(whole, whole, send, recv, twin)

    def cross_copy(c):
        return remote(
            own_ref.at[pl.ds(c * size, size)],
            wide_ref.at[pl.ds(4 * xh * rows + c * size, size)],
            cross_s, cross_r.at[c], opposite,
        )

    def along_copy(c):
        return remote(
            wide_ref.at[pl.ds(across_at + c * size, size)],
            wide_ref.at[pl.ds(along_at + c * size, size)],
            along_s, along_r.at[c], onward,
        )

    def twin_copy(c):
        return remote(
            wide_ref.at[pl.ds(twin_from + c * size, size)],
            wide_ref.at[pl.ds(twin_to + c * size, size)],
            twin_s, twin_r, twin,
        )

    def own_copy():
        return remote(own_ref, wide_ref.at[pl.ds(own_to, rows)], own_s, own_r, twin)

    def every(count, do):
        def step(k, c):
            do(k)
            return c

        lax.fori_loop(0, count, step, 0)

    for i in range(4):
        place_copy(i).start()
    for c in range(chunks):
        cross_copy(c).start()
    own_copy().start()
    wide_ref[pl.ds(2 * rows, rows)] = own_ref[...]
    local_ref[...] = jnp.zeros_like(local_ref)
    image_ref[0] = jnp.zeros((BS, rank), F32)

    line = lax.broadcasted_iota(jnp.int32, (1, 8, BS), 1)
    w = jnp.where(line == 0, ranges[0], jnp.where(line == 1, ranges[1], ranges[2]))
    w = LOG2E / w
    w = jnp.where(line < 3, w * w, 0.0)

    def spread(ref_value, step):
        even = ref_value.astype(F32).reshape(rows // 2, 8, BS)
        odd = jnp.concatenate([even[:, 4:], even[:, :4]], axis=1)
        both = jnp.stack([even, odd], axis=1).reshape(rows, 8, BS)
        both = both + jnp.where(line == 0, 8.0 * (step - 2) - 4.0, 0.0)
        norm = jnp.sum(both * both * w, axis=1, keepdims=True)
        return both, norm

    def put_right(both, norm, step):
        n1, n2, n3 = pieces(norm)
        tail = jnp.where(line == 4, n1, jnp.where(line == 5, n2, jnp.where(line == 6, n3, 0.0)))
        base = jnp.where(line < 4, both, tail)
        twice = jnp.concatenate([base, base], axis=1).astype(BF16)
        right_ref[pl.ds(step * rows, rows)] = twice

    both, norm = spread(point_ref[...], 2)
    put_right(both, norm, 2)
    full = jnp.where(line < 3, -2.0 * w * both, jnp.where(line == 3, norm, 0.0))
    a1, a2, a3 = pieces(full)
    a1 = a1 + jnp.where(jnp.logical_and(line > 3, line < 7), 1.0, 0.0)
    left_ref[...] = jnp.concatenate([a1, a2, a3, jnp.zeros_like(a1)], axis=1)
    all_places().wait_recv()
    for step in (0, 1, 3, 4):
        both, norm = spread(place_ref[step], step)
        put_right(both, norm, step)

    def left_of(g):
        return jnp.transpose(left_ref[g]).astype(BF16)

    def block_pair(left, g, n):
        right = jnp.concatenate([right_ref[column(g, n)], right_ref[column(g, n + 1)]], axis=1)
        right = jnp.concatenate([right, right], axis=0)
        square = jnp.dot(left, right, preferred_element_type=F32)
        square = jnp.maximum(square, 1e-10)
        rest = CUTOFF * LOG2E - square * lax.rsqrt(square)
        taper = jnp.maximum(rest, 0.0)
        return (jnp.exp2(rest) * taper * taper).astype(BF16)

    def build(g):
        left = left_of(g)
        for n in range(0, slots, 2):
            early_ref[g, :, n * BS : (n + 2) * BS] = block_pair(left, g, n)

    early = early_ref.shape[0]
    late = late_ref.shape[0]
    share = early // late
    lag = 2
    paced = early - 2 * lag

    def turn(c, carry):
        def row(g, carry):
            build(g)
            return carry

        lax.fori_loop((c * paced) // chunks, ((c + 1) * paced) // chunks, row, 0)
        cross_copy(c).wait_recv()
        along_copy(c).start()

        @pl.when(c >= lag)
        def _():
            along_copy(c - lag).wait_recv()
            twin_copy(c - lag).start()

        return carry

    lax.fori_loop(0, chunks, turn, 0)

    def tail(i):
        every(2, lambda j: build(paced + 2 * i + j))
        along_copy(chunks - lag + i).wait_recv()
        twin_copy(chunks - lag + i).start()

    every(lag, tail)
    own_copy().wait_recv()
    all_rows(twin_s, twin_r).wait_recv()

    factor = math.exp(-CUTOFF) / (8.0 * (CUTOFF * LOG2E) ** 2)

    def out_copy(g):
        return pltpu.make_async_copy(image_ref.at[g + 1], image_hbm.at[g], out_sem)

    def add_gram(image):
        high = image.astype(BF16)
        low = (image - high.astype(F32)).astype(BF16)
        pair = jnp.concatenate([high, low], axis=1)
        local_ref[...] += lax.dot_general(
            high, pair, (((0,), (0,)), ((), ())), preferred_element_type=F32
        )

    def multiply(g, source, at, beside):
        add_gram(image_ref[g])
        acc = jnp.zeros((BS, rank), F32)
        for n in range(0, slots, 2):
            parts = jnp.concatenate([wide_ref[column(g, n)], wide_ref[column(g, n + 1)]], axis=0)
            beside()
            acc = acc + jnp.dot(
                source[at, :, n * BS : (n + 2) * BS], parts, preferred_element_type=F32
            )
        image = acc * factor + NUGGET * own_ref[g].astype(F32)
        image_ref[g + 1] = image
        out_copy(g).start()

    def both_at_once(t):
        left = left_of(early + t)
        done = [0, 0]

        def beside():
            if done[0] % share == 0:
                n = 2 * done[1]
                late_ref[t, :, n * BS : (n + 2) * BS] = block_pair(left, early + t, n)
                done[1] += 1
            done[0] += 1

        for i in range(share):
            g = t * share + i
            multiply(g, early_ref, g, beside)

    every(late, both_at_once)
    every(late, lambda t: multiply(early + t, late_ref, t, lambda: None))
    add_gram(image_ref[rows])
    cross = local_ref[:, rank:]
    part = local_ref[:, :rank] + cross + jnp.transpose(cross)
    part_ref[...] = part.reshape(part_ref.shape)

    def copy1(k):
        p, device = peer_a(k)
        return remote(part_ref.at[p], got1.at[a], s1, r1, device)

    def copy2(k):
        return remote(one_sum, got2.at[y], s2, r2, peer_y(k))

    def copy3(k):
        return remote(two_sum, got3.at[z], s3, r3, peer_z(k))

    def copy4(k):
        return remote(three_sum, got4.at[a], s4, r4, peer_a(k)[1])

    def all_pieces(got, count, send, recv):
        pieces_of_others = got.at[pl.ds(0, count - 1)]
        return remote(pieces_of_others, pieces_of_others, send, recv, twin)

    def exchange(copy, count, own, value, got, send, recv):
        for k in range(1, count):
            copy(k).start()
        got[own] = value
        all_pieces(got, count, send, recv).wait_recv()

    exchange(copy1, 8, a, part_ref[a], got1, s1, r1)
    one_sum[...] = jnp.sum(got1[...], axis=0)
    exchange(copy2, 4, y, one_sum[...], got2, s2, r2)
    two_sum[...] = jnp.sum(got2[...], axis=0)
    exchange(copy3, 8, z, two_sum[...], got3, s3, r3)
    three_sum[...] = jnp.sum(got3[...], axis=0) * (1.0 / total)
    exchange(copy4, 8, a, three_sum[...], got4, s4, r4)
    gram_ref[...] = got4[...]

    pltpu.make_async_copy(image_ref.at[pl.ds(1, rows)], image_hbm, out_sem).wait()
    all_places().wait_send()
    own_copy().wait_send()
    for send in (cross_s, along_s, twin_s):
        all_rows(send, own_r).wait_send()
    for got, count, send, recv in (
        (got1, 8, s1, r1), (got2, 4, s2, r2), (got3, 8, s3, r3), (got4, 8, s4, r4),
    ):
        all_pieces(got, count, send, recv).wait_send()


def image_and_gram(near, ranges, coords, own, slabs, total):
    rows, size, rank = own.shape
    slots = near.shape[1]
    chunks = 8
    late = rows // 4
    early = rows - late
    vmem = pl.BlockSpec(memory_space=pltpu.VMEM)
    smem = pl.BlockSpec(memory_space=pltpu.SMEM)
    dma = pltpu.SemaphoreType.DMA
    piece = rank // 8
    image, gram = pl.pallas_call(
        functools.partial(image_kernel, total, slabs),
        name="image",
        out_shape=(
            jax.ShapeDtypeStruct((rows, size, rank), F32),
            jax.ShapeDtypeStruct((8, piece, rank), F32),
        ),
        in_specs=[smem, smem, vmem, vmem],
        out_specs=(pl.BlockSpec(memory_space=pl.ANY), vmem),
        scratch_shapes=[
            pltpu.VMEM((early, size, slots * size), BF16),
            pltpu.VMEM((late, size, slots * size), BF16),
            pltpu.VMEM((rows + 1, size, rank), F32),
            pltpu.VMEM((STEPS * rows, size, rank), BF16),
            pltpu.VMEM((STEPS, rows * 4, size), BF16),
            pltpu.VMEM((rows * 4, size), BF16),
            pltpu.VMEM((rows * 4, size), F32),
            pltpu.VMEM((STEPS * rows, 16, size), BF16),
            pltpu.VMEM((rows, 32, size), F32),
            pltpu.VMEM((rank, 2 * rank), F32),
        ]
        + [pltpu.VMEM((n, piece, rank), F32) for n in (8, 8, 4, 8, 8)]
        + [pltpu.VMEM((piece, rank), F32)] * 3
        + [dma(())] * 2
        + [dma(()), dma((chunks,))] * 2
        + [dma(())] * 12
        + [dma(())],
        compiler_params=pltpu.CompilerParams(
            collective_id=1, has_side_effects=True, vmem_limit_bytes=58 << 20
        ),
    )(near, ranges, coords, own)
    return image, gram.reshape(rank, rank)


def nt(a, b):
    return lax.dot_general(
        a, b, (((1,), (1,)), ((), ())), precision=HIGHEST, preferred_element_type=F32
    )


def nn(a, b):
    return jnp.dot(a, b, precision=HIGHEST, preferred_element_type=F32)


def basis_kernel(
    gram_ref, image_hbm, basis_hbm, factor_ref, inverse_ref, work_ref, image_ref, out_ref,
    in_sem, out_sem,
):
    n = gram_ref.shape[0]
    chunks = out_sem.shape[0]
    size = image_ref.shape[0] // chunks
    fetch = pltpu.make_async_copy(image_hbm, image_ref, in_sem)
    fetch.start()

    row = lax.broadcasted_iota(jnp.int32, (n, n), 0)
    col = lax.broadcasted_iota(jnp.int32, (n, n), 1)
    diag = row == col
    weight = jnp.where(row > col, 1.0, jnp.where(diag, 0.5, 0.0)).astype(F32)
    eye = jnp.where(diag, 1.0, 0.0).astype(F32)
    gram = gram_ref[...]
    only = jnp.where(diag, gram, 0.0)
    down = lax.rsqrt(jnp.sum(only, axis=1, keepdims=True))
    across = lax.rsqrt(jnp.sum(only, axis=0, keepdims=True))
    first = gram * down * across - eye
    inverse_ref[...] = (eye - first * weight) * across

    def unsettled(state):
        size, turn = state
        return jnp.logical_and(jnp.logical_not(size < 1e-6), turn < 8)

    def refine(state):
        turn = state[1]
        x = inverse_ref[...]
        gap = nt(nn(x, gram_ref[...]), x) - eye
        inverse_ref[...] = x - nn(gap * weight, x)
        return jnp.sum(gap * gap), turn + 1

    far, _ = lax.while_loop(unsettled, refine, (jnp.sum(first * first), jnp.int32(0)))
    settled = far < 1e-6

    @pl.when(settled)
    def _():
        factor_ref[...] = jnp.where(row <= col, nn(inverse_ref[...], gram_ref[...]), 0.0)

    @pl.when(jnp.logical_not(settled))
    def _():
        work_ref[:, :n] = gram_ref[...]
        work_ref[:, n:] = eye
        wide = lax.broadcasted_iota(jnp.int32, (n, 2 * n), 1)
        tall = lax.broadcasted_iota(jnp.int32, (n, 1), 0)

        def eliminate(k, c):
            m = work_ref[...]
            pivot_row = jnp.sum(jnp.where(tall == k, m, 0.0), axis=0, keepdims=True)
            column = jnp.sum(jnp.where(wide == k, m, 0.0), axis=1, keepdims=True)
            pivot = jnp.sum(jnp.where(tall == k, column, 0.0), axis=0, keepdims=True)
            ratio = jnp.where(tall > k, column / pivot, 0.0)
            work_ref[...] = m - ratio * pivot_row
            return c

        lax.fori_loop(0, n, eliminate, 0)
        upper = work_ref[:, :n]
        scale = lax.rsqrt(jnp.sum(jnp.where(diag, upper, 0.0), axis=1, keepdims=True))
        factor_ref[...] = jnp.where(row <= col, upper * scale, 0.0)
        inverse_ref[...] = work_ref[:, n:] * scale

    x = jnp.transpose(inverse_ref[...])
    xh = x.astype(BF16)
    xl = (x - xh.astype(F32)).astype(BF16)
    right = jnp.concatenate(
        [
            jnp.concatenate([xh, xl], axis=1),
            jnp.concatenate([xh, jnp.zeros_like(xl)], axis=1),
        ],
        axis=0,
    )
    fetch.wait()

    def send(i):
        piece = pl.ds(i * size, size)
        return pltpu.make_async_copy(out_ref.at[piece], basis_hbm.at[piece], out_sem.at[i])

    for i in range(chunks):
        image = image_ref[i * size : (i + 1) * size]
        high = image.astype(BF16)
        low = (image - high.astype(F32)).astype(BF16)
        both = jnp.concatenate([high, low], axis=1)
        product = jnp.dot(both, right, preferred_element_type=F32)
        out_ref[i * size : (i + 1) * size] = product[:, :n] + product[:, n:]
        send(i).start()
    for i in range(chunks):
        send(i).wait()


def basis_and_factor(gram, image):
    n = gram.shape[0]
    rows = image.shape[0]
    chunks = 8
    vmem = pl.BlockSpec(memory_space=pltpu.VMEM)
    hbm = pl.BlockSpec(memory_space=pl.ANY)
    return pl.pallas_call(
        basis_kernel,
        name="basis",
        out_shape=(
            jax.ShapeDtypeStruct((rows, n), F32),
            jax.ShapeDtypeStruct((n, n), F32),
        ),
        in_specs=[vmem, hbm],
        out_specs=(hbm, vmem),
        scratch_shapes=[
            pltpu.VMEM((n, n), F32),
            pltpu.VMEM((n, 2 * n), F32),
            pltpu.VMEM((rows, n), F32),
            pltpu.VMEM((rows, n), F32),
            pltpu.SemaphoreType.DMA(()),
            pltpu.SemaphoreType.DMA((chunks,)),
        ],
    )(gram, image)


def on_device(panel, coords, neighbours, ranges):
    block_count = neighbours.shape[0]
    block_size = panel.shape[0] // block_count
    width = panel.shape[1]
    sector_count = lax.axis_size("sector")
    slab_count = lax.axis_size("depth")
    blocked = panel.reshape(block_count, block_size, width)

    total_cells = float(panel.shape[0] * sector_count * slab_count)
    image, gram = image_and_gram(
        neighbours, ranges, coords, blocked, slab_count, total_cells
    )
    image = image.reshape(block_count * block_size, width)
    basis, factor = basis_and_factor(gram, image)
    return (basis, factor)


def solution(mesh):
    in_specs = (
        P(("sector", "depth"), None),
        P(None, ("sector", "depth")),
        P(("sector", "depth"), None),
        P(),
    )
    out_specs = (P(("sector", "depth"), None), P())
    return jax.shard_map(
        on_device, mesh=mesh, in_specs=in_specs, out_specs=out_specs, check_vma=False
    )
```

```python
import functools
import math

import jax
import jax.numpy as jnp
from jax import lax
from jax.experimental import pallas as pl
from jax.experimental.pallas import tpu as pltpu
from jax.sharding import PartitionSpec as P

AZ_SEC = 8
DZ = 8
CUTOFF = 3.0
NUGGET = 0.5
BS = 128
LOG2E = 1.4426950408889634
MESH = pl.DeviceIdType.MESH
F32 = jnp.float32
BF16 = jnp.bfloat16
HIGHEST = lax.Precision.HIGHEST


STEPS = 5


def place():
    s = lax.axis_index("sector")
    d = lax.axis_index("depth")
    return s // 4, (s // 2) % 2, s % 2, d // 8, d % 8


def short(value):
    return value.astype(BF16).astype(F32)


def pieces(value):
    one = short(value)
    two = short(value - one)
    return one, two, value - one - two


def image_kernel(
    total, slabs, near, ranges, coords_ref, own_ref, image_hbm, gram_ref,
    early_ref, late_ref, image_ref, wide_ref, place_ref, mine_ref, point_ref, right_ref, left_ref, local_ref,
    part_ref, got1, got2, got3, got4, one_sum, two_sum, three_sum,
    place_s, place_r, cross_s, cross_r, along_s, along_r, twin_s, twin_r, own_s, own_r,
    s1, r1, s2, r2, s3, r3, s4, r4, out_sem, own_in_sem,
):
    rows, rank = own_ref.shape[0], own_ref.shape[2]
    slots = near.shape[1]
    size = rows // 8
    main = 7
    ends = [(7 * size, size // 2), (7 * size + size // 2, size // 4), (8 * size - size // 4, size // 4)]
    y, xh, core, xl, z = place()
    s = lax.axis_index("sector")
    d = lax.axis_index("depth")
    x = xh * 2 + xl
    a = core * 4 + x

    def sector(k):
        return lax.rem(s + k + 16, 16), d

    def peer_a(k):
        p = lax.rem(a + k, 8)
        px = lax.rem(p, 4)
        return p, (y * 4 + (px // 2) * 2 + p // 4, lax.rem(px, 2) * 8 + z)

    def peer_y(k):
        return lax.rem(s + 4 * k, 16), d

    def peer_z(k):
        return s, xl * 8 + lax.rem(z + k, 8)

    barrier = pltpu.get_barrier_semaphore()
    greeted = [sector(k) for k in (-2, -1, 1, 2)]
    greeted += [peer_y(k) for k in range(1, 4)]
    greeted += [peer_a(k)[1] for k in range(1, 8)] + [peer_z(k) for k in range(1, 8)]
    for device in greeted:
        pl.semaphore_signal(barrier, inc=1, device_id=device, device_id_type=MESH)

    corner = lax.broadcasted_iota(jnp.int32, (3, 1), 0)
    corner = jnp.where(corner == 0, s * AZ_SEC, jnp.where(corner == 1, 32, d * DZ + DZ // 2))
    point_ref[...] = jnp.ones_like(point_ref)
    for g in range(rows):
        inside = coords_ref[:, g * BS : (g + 1) * BS] - corner
        point_ref[4 * g : 4 * g + 3, :] = inside.astype(F32)
    mine_ref[...] = point_ref[...].astype(BF16)

    shift = (slabs * rows).bit_length() - 1

    def column(g, n):
        block = near[g, n]
        step = lax.rem(lax.shift_right_logical(block, shift) - s + 18, 16)
        return jnp.minimum(step, STEPS - 1) * rows + lax.rem(block, rows)

    pl.semaphore_wait(barrier, len(greeted))

    opposite = sector(2 - 4 * xh)
    onward = sector(4 - 8 * xh)
    across_at = (4 - 4 * xh) * rows
    along_at = 4 * xh * rows
    twin = sector(1 - 2 * core)
    twin_from = (4 - 4 * core) * rows
    twin_to = (3 - 2 * core) * rows
    own_to = (1 + 2 * core) * rows

    def remote(src, dst, send, recv, dev):
        return pltpu.make_async_remote_copy(
            src, dst, send, recv, device_id=dev, device_id_type=MESH
        )

    def place_cross():
        return remote(mine_ref, place_ref.at[4 * xh], place_s.at[0], place_r.at[0], opposite)

    def place_along():
        return remote(
            place_ref.at[4 - 4 * xh], place_ref.at[4 * xh], place_s.at[1], place_r.at[1], onward
        )

    def place_own():
        return remote(mine_ref, place_ref.at[1 + 2 * core], place_s.at[2], place_r.at[2], twin)

    def place_twin():
        return remote(
            place_ref.at[4 - 4 * core], place_ref.at[3 - 2 * core],
            place_s.at[3], place_r.at[3], twin,
        )

    def all_rows(send, recv):
        whole = wide_ref.at[pl.ds(0, rows)]
        return remote(whole, whole, send, recv, twin)

    def span(c):
        return (c * size, size) if not isinstance(c, int) or c < main else ends[c - main]

    def cross_copy(c):
        start, count = span(c)
        return remote(
            own_ref.at[pl.ds(start, count)],
            wide_ref.at[pl.ds(4 * xh * rows + start, count)],
            cross_s, cross_r.at[c], opposite,
        )

    def along_copy(c):
        start, count = span(c)
        return remote(
            wide_ref.at[pl.ds(across_at + start, count)],
            wide_ref.at[pl.ds(along_at + start, count)],
            along_s, along_r.at[c], onward,
        )

    def twin_copy(c):
        start, count = span(c)
        return remote(
            wide_ref.at[pl.ds(twin_from + start, count)],
            wide_ref.at[pl.ds(twin_to + start, count)],
            twin_s, twin_r, twin,
        )

    def own_in():
        return pltpu.make_async_copy(own_ref, wide_ref.at[pl.ds(2 * rows, rows)], own_in_sem)

    def own_copy():
        return remote(own_ref, wide_ref.at[pl.ds(own_to, rows)], own_s, own_r, twin)

    def every(count, do):
        def step(k, c):
            do(k)
            return c

        lax.fori_loop(0, count, step, 0)

    place_cross().start()
    place_own().start()
    for c in range(main + len(ends)):
        cross_copy(c).start()
    own_in().start()
    local_ref[...] = jnp.zeros_like(local_ref)
    image_ref[0] = jnp.zeros((BS, rank), F32)

    line = lax.broadcasted_iota(jnp.int32, (1, 8, BS), 1)
    w = jnp.where(line == 0, ranges[0], jnp.where(line == 1, ranges[1], ranges[2]))
    w = LOG2E / w
    w = jnp.where(line < 3, w * w, 0.0)

    def spread(ref_value, step):
        even = ref_value.astype(F32).reshape(rows // 2, 8, BS)
        odd = jnp.concatenate([even[:, 4:], even[:, :4]], axis=1)
        both = jnp.stack([even, odd], axis=1).reshape(rows, 8, BS)
        both = both + jnp.where(line == 0, 8.0 * (step - 2) - 4.0, 0.0)
        norm = jnp.sum(both * both * w, axis=1, keepdims=True)
        return both, norm

    def put_right(both, norm, step):
        n1, n2, n3 = pieces(norm)
        tail = jnp.where(line == 4, n1, jnp.where(line == 5, n2, jnp.where(line == 6, n3, 0.0)))
        base = jnp.where(line < 4, both, tail)
        twice = jnp.concatenate([base, base], axis=1).astype(BF16)
        right_ref[pl.ds(step * rows, rows)] = twice

    both, norm = spread(point_ref[...], 2)
    put_right(both, norm, 2)
    full = jnp.where(line < 3, -2.0 * w * both, jnp.where(line == 3, norm, 0.0))
    a1, a2, a3 = pieces(full)
    a1 = a1 + jnp.where(jnp.logical_and(line > 3, line < 7), 1.0, 0.0)
    left_ref[...] = jnp.concatenate([a1, a2, a3, jnp.zeros_like(a1)], axis=1)
    place_cross().wait_recv()
    place_along().start()
    place_along().wait_recv()
    place_twin().start()
    own_copy().start()
    place_own().wait_recv()
    place_twin().wait_recv()
    for step in (0, 1, 3, 4):
        both, norm = spread(place_ref[step], step)
        put_right(both, norm, step)

    def left_of(g):
        return jnp.transpose(left_ref[g]).astype(BF16)

    def block_pair(left, g, n):
        right = jnp.concatenate([right_ref[column(g, n)], right_ref[column(g, n + 1)]], axis=1)
        right = jnp.concatenate([right, right], axis=0)
        square = jnp.dot(left, right, preferred_element_type=F32)
        square = jnp.maximum(square, 1e-10)
        rest = CUTOFF * LOG2E - square * lax.rsqrt(square)
        taper = jnp.maximum(rest, 0.0)
        return (jnp.exp2(rest) * taper * taper).astype(BF16)

    def build(g):
        left = left_of(g)
        for n in range(0, slots, 2):
            early_ref[g, :, n * BS : (n + 2) * BS] = block_pair(left, g, n)

    early = early_ref.shape[0]
    late = late_ref.shape[0]
    share = early // late
    lag = 2
    paced = early - 5

    def turn(c, carry):
        def row(g, carry):
            build(g)
            return carry

        lax.fori_loop((c * paced) // main, ((c + 1) * paced) // main, row, 0)
        cross_copy(c).wait_recv()
        along_copy(c).start()

        @pl.when(c >= lag)
        def _():
            along_copy(c - lag).wait_recv()
            twin_copy(c - lag).start()

        return carry

    lax.fori_loop(0, main, turn, 0)

    def onto_twin(c):
        along_copy(c).wait_recv()
        twin_copy(c).start()

    for i in range(len(ends)):
        build(paced + i)
        cross_copy(main + i).wait_recv()
        along_copy(main + i).start()
        if i < lag:
            onto_twin(main - lag + i)
    every(2, lambda j: build(paced + 3 + j))
    for i in range(len(ends)):
        onto_twin(main + i)
    own_in().wait()
    own_copy().wait_recv()
    all_rows(twin_s, twin_r).wait_recv()

    factor = math.exp(-CUTOFF) / (8.0 * (CUTOFF * LOG2E) ** 2)

    def out_copy(g):
        return pltpu.make_async_copy(image_ref.at[g + 1], image_hbm.at[g], out_sem)

    def add_gram(image):
        high = image.astype(BF16)
        low = (image - high.astype(F32)).astype(BF16)
        pair = jnp.concatenate([high, low], axis=1)
        local_ref[...] += lax.dot_general(
            high, pair, (((0,), (0,)), ((), ())), preferred_element_type=F32
        )

    def multiply(g, source, at, beside):
        add_gram(image_ref[g])
        acc = jnp.zeros((BS, rank), F32)
        for n in range(0, slots, 2):
            parts = jnp.concatenate([wide_ref[column(g, n)], wide_ref[column(g, n + 1)]], axis=0)
            beside()
            acc = acc + jnp.dot(
                source[at, :, n * BS : (n + 2) * BS], parts, preferred_element_type=F32
            )
        image = acc * factor + NUGGET * wide_ref[2 * rows + g].astype(F32)
        image_ref[g + 1] = image
        out_copy(g).start()

    def both_at_once(t):
        left = left_of(early + t)
        done = [0, 0]

        def beside():
            if done[0] % share == 0:
                n = 2 * done[1]
                late_ref[t, :, n * BS : (n + 2) * BS] = block_pair(left, early + t, n)
                done[1] += 1
            done[0] += 1

        for i in range(share):
            g = t * share + i
            multiply(g, early_ref, g, beside)

    every(late, both_at_once)
    every(late, lambda t: multiply(early + t, late_ref, t, lambda: None))
    add_gram(image_ref[rows])
    cross = local_ref[:, rank:]
    part = local_ref[:, :rank] + cross + jnp.transpose(cross)
    part_ref[...] = part.reshape(part_ref.shape)

    def copy1(k):
        p, device = peer_a(k)
        return remote(part_ref.at[p], got1.at[a], s1, r1, device)

    def copy2(k):
        return remote(one_sum, got2.at[y], s2, r2, peer_y(k))

    def copy3(k):
        return remote(two_sum, got3.at[z], s3, r3, peer_z(k))

    def copy4(k):
        return remote(three_sum, got4.at[a], s4, r4, peer_a(k)[1])

    def all_pieces(got, count, send, recv):
        pieces_of_others = got.at[pl.ds(0, count - 1)]
        return remote(pieces_of_others, pieces_of_others, send, recv, twin)

    def exchange(copy, count, own, value, got, send, recv):
        for k in range(1, count):
            copy(k).start()
        got[own] = value
        all_pieces(got, count, send, recv).wait_recv()

    exchange(copy1, 8, a, part_ref[a], got1, s1, r1)
    one_sum[...] = jnp.sum(got1[...], axis=0)
    exchange(copy2, 4, y, one_sum[...], got2, s2, r2)
    two_sum[...] = jnp.sum(got2[...], axis=0)
    exchange(copy3, 8, z, two_sum[...], got3, s3, r3)
    three_sum[...] = jnp.sum(got3[...], axis=0) * (1.0 / total)
    exchange(copy4, 8, a, three_sum[...], got4, s4, r4)
    gram_ref[...] = got4[...]

    pltpu.make_async_copy(image_ref.at[pl.ds(1, rows)], image_hbm, out_sem).wait()
    for copy in (place_cross, place_along, place_own, place_twin):
        copy().wait_send()
    own_copy().wait_send()
    for send in (cross_s, along_s, twin_s):
        all_rows(send, own_r).wait_send()
    for got, count, send, recv in (
        (got1, 8, s1, r1), (got2, 4, s2, r2), (got3, 8, s3, r3), (got4, 8, s4, r4),
    ):
        all_pieces(got, count, send, recv).wait_send()


def image_and_gram(near, ranges, coords, own, slabs, total):
    rows, size, rank = own.shape
    slots = near.shape[1]
    late = rows // 4
    early = rows - late
    vmem = pl.BlockSpec(memory_space=pltpu.VMEM)
    smem = pl.BlockSpec(memory_space=pltpu.SMEM)
    dma = pltpu.SemaphoreType.DMA
    piece = rank // 8
    image, gram = pl.pallas_call(
        functools.partial(image_kernel, total, slabs),
        name="image",
        out_shape=(
            jax.ShapeDtypeStruct((rows, size, rank), F32),
            jax.ShapeDtypeStruct((8, piece, rank), F32),
        ),
        in_specs=[smem, smem, vmem, pl.BlockSpec(memory_space=pl.ANY)],
        out_specs=(pl.BlockSpec(memory_space=pl.ANY), vmem),
        scratch_shapes=[
            pltpu.VMEM((early, size, slots * size), BF16),
            pltpu.VMEM((late, size, slots * size), BF16),
            pltpu.VMEM((rows + 1, size, rank), F32),
            pltpu.VMEM((STEPS * rows, size, rank), BF16),
            pltpu.VMEM((STEPS, rows * 4, size), BF16),
            pltpu.VMEM((rows * 4, size), BF16),
            pltpu.VMEM((rows * 4, size), F32),
            pltpu.VMEM((STEPS * rows, 16, size), BF16),
            pltpu.VMEM((rows, 32, size), F32),
            pltpu.VMEM((rank, 2 * rank), F32),
        ]
        + [pltpu.VMEM((n, piece, rank), F32) for n in (8, 8, 4, 8, 8)]
        + [pltpu.VMEM((piece, rank), F32)] * 3
        + [dma((4,))] * 2
        + [dma(()), dma((10,))] * 2
        + [dma(())] * 14,
        compiler_params=pltpu.CompilerParams(
            collective_id=1, has_side_effects=True, vmem_limit_bytes=58 << 20
        ),
    )(near, ranges, coords, own)
    return image, gram.reshape(rank, rank)


def nt(a, b):
    return lax.dot_general(
        a, b, (((1,), (1,)), ((), ())), precision=HIGHEST, preferred_element_type=F32
    )


def nn(a, b):
    return jnp.dot(a, b, precision=HIGHEST, preferred_element_type=F32)


def basis_kernel(
    gram_ref, image_hbm, basis_hbm, factor_ref, inverse_ref, work_ref, image_ref, out_ref,
    in_sem, out_sem,
):
    n = gram_ref.shape[0]
    chunks = out_sem.shape[0]
    size = image_ref.shape[0] // chunks
    fetch = pltpu.make_async_copy(image_hbm, image_ref, in_sem)
    fetch.start()

    row = lax.broadcasted_iota(jnp.int32, (n, n), 0)
    col = lax.broadcasted_iota(jnp.int32, (n, n), 1)
    diag = row == col
    weight = jnp.where(row > col, 1.0, jnp.where(diag, 0.5, 0.0)).astype(F32)
    eye = jnp.where(diag, 1.0, 0.0).astype(F32)
    gram = gram_ref[...]
    only = jnp.where(diag, gram, 0.0)
    down = lax.rsqrt(jnp.sum(only, axis=1, keepdims=True))
    across = lax.rsqrt(jnp.sum(only, axis=0, keepdims=True))
    first = gram * down * across - eye
    inverse_ref[...] = (eye - first * weight) * across

    def unsettled(state):
        size, turn = state
        return jnp.logical_and(jnp.logical_not(size < 1e-6), turn < 8)

    def refine(state):
        turn = state[1]
        x = inverse_ref[...]
        gap = nt(nn(x, gram_ref[...]), x) - eye
        inverse_ref[...] = x - nn(gap * weight, x)
        return jnp.sum(gap * gap), turn + 1

    far, _ = lax.while_loop(unsettled, refine, (jnp.sum(first * first), jnp.int32(0)))
    settled = far < 1e-6

    @pl.when(settled)
    def _():
        factor_ref[...] = jnp.where(row <= col, nn(inverse_ref[...], gram_ref[...]), 0.0)

    @pl.when(jnp.logical_not(settled))
    def _():
        work_ref[:, :n] = gram_ref[...]
        work_ref[:, n:] = eye
        wide = lax.broadcasted_iota(jnp.int32, (n, 2 * n), 1)
        tall = lax.broadcasted_iota(jnp.int32, (n, 1), 0)

        def eliminate(k, c):
            m = work_ref[...]
            pivot_row = jnp.sum(jnp.where(tall == k, m, 0.0), axis=0, keepdims=True)
            column = jnp.sum(jnp.where(wide == k, m, 0.0), axis=1, keepdims=True)
            pivot = jnp.sum(jnp.where(tall == k, column, 0.0), axis=0, keepdims=True)
            ratio = jnp.where(tall > k, column / pivot, 0.0)
            work_ref[...] = m - ratio * pivot_row
            return c

        lax.fori_loop(0, n, eliminate, 0)
        upper = work_ref[:, :n]
        scale = lax.rsqrt(jnp.sum(jnp.where(diag, upper, 0.0), axis=1, keepdims=True))
        factor_ref[...] = jnp.where(row <= col, upper * scale, 0.0)
        inverse_ref[...] = work_ref[:, n:] * scale

    x = jnp.transpose(inverse_ref[...])
    xh = x.astype(BF16)
    xl = (x - xh.astype(F32)).astype(BF16)
    right = jnp.concatenate(
        [
            jnp.concatenate([xh, xl], axis=1),
            jnp.concatenate([xh, jnp.zeros_like(xl)], axis=1),
        ],
        axis=0,
    )
    fetch.wait()

    def send(i):
        piece = pl.ds(i * size, size)
        return pltpu.make_async_copy(out_ref.at[piece], basis_hbm.at[piece], out_sem.at[i])

    for i in range(chunks):
        image = image_ref[i * size : (i + 1) * size]
        high = image.astype(BF16)
        low = (image - high.astype(F32)).astype(BF16)
        both = jnp.concatenate([high, low], axis=1)
        product = jnp.dot(both, right, preferred_element_type=F32)
        out_ref[i * size : (i + 1) * size] = product[:, :n] + product[:, n:]
        send(i).start()
    for i in range(chunks):
        send(i).wait()


def basis_and_factor(gram, image):
    n = gram.shape[0]
    rows = image.shape[0]
    chunks = 8
    vmem = pl.BlockSpec(memory_space=pltpu.VMEM)
    hbm = pl.BlockSpec(memory_space=pl.ANY)
    return pl.pallas_call(
        basis_kernel,
        name="basis",
        out_shape=(
            jax.ShapeDtypeStruct((rows, n), F32),
            jax.ShapeDtypeStruct((n, n), F32),
        ),
        in_specs=[vmem, hbm],
        out_specs=(hbm, vmem),
        scratch_shapes=[
            pltpu.VMEM((n, n), F32),
            pltpu.VMEM((n, 2 * n), F32),
            pltpu.VMEM((rows, n), F32),
            pltpu.VMEM((rows, n), F32),
            pltpu.SemaphoreType.DMA(()),
            pltpu.SemaphoreType.DMA((chunks,)),
        ],
    )(gram, image)


def on_device(panel, coords, neighbours, ranges):
    block_count = neighbours.shape[0]
    block_size = panel.shape[0] // block_count
    width = panel.shape[1]
    sector_count = lax.axis_size("sector")
    slab_count = lax.axis_size("depth")
    blocked = panel.reshape(block_count, block_size, width)

    total_cells = float(panel.shape[0] * sector_count * slab_count)
    image, gram = image_and_gram(
        neighbours, ranges, coords, blocked, slab_count, total_cells
    )
    image = image.reshape(block_count * block_size, width)
    basis, factor = basis_and_factor(gram, image)
    return (basis, factor)


def solution(mesh):
    in_specs = (
        P(("sector", "depth"), None),
        P(None, ("sector", "depth")),
        P(("sector", "depth"), None),
        P(),
    )
    out_specs = (P(("sector", "depth"), None), P())
    return jax.shard_map(
        on_device, mesh=mesh, in_specs=in_specs, out_specs=out_specs, check_vma=False
    )
```

```python
import functools
import math

import jax
import jax.numpy as jnp
from jax import lax
from jax.experimental import pallas as pl
from jax.experimental.pallas import tpu as pltpu
from jax.sharding import PartitionSpec as P

AZ_SEC = 8
DZ = 8
CUTOFF = 3.0
NUGGET = 0.5
BS = 128
LOG2E = 1.4426950408889634
MESH = pl.DeviceIdType.MESH
F32 = jnp.float32
BF16 = jnp.bfloat16
HIGHEST = lax.Precision.HIGHEST


STEPS = 5


def place():
    s = lax.axis_index("sector")
    d = lax.axis_index("depth")
    return s // 4, (s // 2) % 2, s % 2, d // 8, d % 8


def short(value):
    return value.astype(BF16).astype(F32)


def pieces(value):
    one = short(value)
    two = short(value - one)
    return one, two, value - one - two


def image_kernel(
    total, slabs, near, ranges, coords_ref, own_ref, image_hbm, gram_ref,
    early_ref, late_ref, image_ref, wide_ref, place_ref, mine_ref, point_ref, right_ref, left_ref, local_ref,
    part_ref, got1, got2, got3, got4, one_sum, two_sum, three_sum,
    place_s, place_r, cross_s, cross_r, along_s, along_r, twin_s, twin_r, own_s, own_r,
    s1, r1, s2, r2, s3, r3, s4, r4, out_sem,
):
    rows, rank = own_ref.shape[0], own_ref.shape[2]
    slots = near.shape[1]
    size = rows // 8
    half = size // 2
    main = 6
    first, last = main, main + 2
    spans = {first: 0, first + 1: half, last: rows - size, last + 1: rows - half}
    y, xh, core, xl, z = place()
    s = lax.axis_index("sector")
    d = lax.axis_index("depth")
    x = xh * 2 + xl
    a = core * 4 + x

    def sector(k):
        return lax.rem(s + k + 16, 16), d

    def peer_a(k):
        p = lax.rem(a + k, 8)
        px = lax.rem(p, 4)
        return p, (y * 4 + (px // 2) * 2 + p // 4, lax.rem(px, 2) * 8 + z)

    def peer_y(k):
        return lax.rem(s + 4 * k, 16), d

    def peer_z(k):
        return s, xl * 8 + lax.rem(z + k, 8)

    barrier = pltpu.get_barrier_semaphore()
    greeted = [sector(k) for k in (-2, -1, 1, 2)]
    greeted += [peer_y(k) for k in range(1, 4)]
    greeted += [peer_a(k)[1] for k in range(1, 8)] + [peer_z(k) for k in range(1, 8)]
    for device in greeted:
        pl.semaphore_signal(barrier, inc=1, device_id=device, device_id_type=MESH)

    corner = lax.broadcasted_iota(jnp.int32, (3, 1), 0)
    corner = jnp.where(corner == 0, s * AZ_SEC, jnp.where(corner == 1, 32, d * DZ + DZ // 2))
    point_ref[...] = jnp.ones_like(point_ref)
    for g in range(rows):
        inside = coords_ref[:, g * BS : (g + 1) * BS] - corner
        point_ref[4 * g : 4 * g + 3, :] = inside.astype(F32)
    mine_ref[...] = point_ref[...].astype(BF16)

    shift = (slabs * rows).bit_length() - 1

    def column(g, n):
        block = near[g, n]
        step = lax.rem(lax.shift_right_logical(block, shift) - s + 18, 16)
        return jnp.minimum(step, STEPS - 1) * rows + lax.rem(block, rows)

    pl.semaphore_wait(barrier, len(greeted))

    opposite = sector(2 - 4 * xh)
    onward = sector(4 - 8 * xh)
    across_at = (4 - 4 * xh) * rows
    along_at = 4 * xh * rows
    twin = sector(1 - 2 * core)
    twin_from = (4 - 4 * core) * rows
    twin_to = (3 - 2 * core) * rows
    own_to = (1 + 2 * core) * rows

    def remote(src, dst, send, recv, dev):
        return pltpu.make_async_remote_copy(
            src, dst, send, recv, device_id=dev, device_id_type=MESH
        )

    def place_copy(i):
        k = (-2, -1, 1, 2)[i]
        return remote(mine_ref, place_ref.at[2 - k], place_s, place_r, sector(k))

    def all_places():
        four = place_ref.at[pl.ds(0, 4)]
        return remote(four, four, place_s, place_r, twin)

    def all_rows(send, recv):
        whole = wide_ref.at[pl.ds(0, rows)]
        return remote(whole, whole, send, recv, twin)

    def span(c):
        return (spans[c], half) if isinstance(c, int) and c >= main else (size + c * size, size)

    def cross_copy(c):
        start, count = span(c)
        return remote(
            own_ref.at[pl.ds(start, count)],
            wide_ref.at[pl.ds(4 * xh * rows + start, count)],
            cross_s, cross_r.at[c], opposite,
        )

    def along_copy(c):
        start, count = span(c)
        return remote(
            wide_ref.at[pl.ds(across_at + start, count)],
            wide_ref.at[pl.ds(along_at + start, count)],
            along_s, along_r.at[c], onward,
        )

    def twin_copy(c):
        start, count = span(c)
        return remote(
            wide_ref.at[pl.ds(twin_from + start, count)],
            wide_ref.at[pl.ds(twin_to + start, count)],
            twin_s, twin_r, twin,
        )

    def own_copy():
        return remote(own_ref, wide_ref.at[pl.ds(own_to, rows)], own_s, own_r, twin)

    def every(count, do):
        def step(k, c):
            do(k)
            return c

        lax.fori_loop(0, count, step, 0)

    for i in range(4):
        place_copy(i).start()
    for c in (first, first + 1, *range(main), last, last + 1):
        cross_copy(c).start()
    own_copy().start()
    wide_ref[pl.ds(2 * rows, rows)] = own_ref[...]
    local_ref[...] = jnp.zeros_like(local_ref)
    image_ref[0] = jnp.zeros((BS, rank), F32)

    line = lax.broadcasted_iota(jnp.int32, (1, 8, BS), 1)
    w = jnp.where(line == 0, ranges[0], jnp.where(line == 1, ranges[1], ranges[2]))
    w = LOG2E / w
    w = jnp.where(line < 3, w * w, 0.0)

    def spread(ref_value, step):
        even = ref_value.astype(F32).reshape(rows // 2, 8, BS)
        odd = jnp.concatenate([even[:, 4:], even[:, :4]], axis=1)
        both = jnp.stack([even, odd], axis=1).reshape(rows, 8, BS)
        both = both + jnp.where(line == 0, 8.0 * (step - 2) - 4.0, 0.0)
        norm = jnp.sum(both * both * w, axis=1, keepdims=True)
        return both, norm

    def put_right(both, norm, step):
        n1, n2, n3 = pieces(norm)
        tail = jnp.where(line == 4, n1, jnp.where(line == 5, n2, jnp.where(line == 6, n3, 0.0)))
        base = jnp.where(line < 4, both, tail)
        twice = jnp.concatenate([base, base], axis=1).astype(BF16)
        right_ref[pl.ds(step * rows, rows)] = twice

    both, norm = spread(point_ref[...], 2)
    put_right(both, norm, 2)
    full = jnp.where(line < 3, -2.0 * w * both, jnp.where(line == 3, norm, 0.0))
    a1, a2, a3 = pieces(full)
    a1 = a1 + jnp.where(jnp.logical_and(line > 3, line < 7), 1.0, 0.0)
    left_ref[...] = jnp.concatenate([a1, a2, a3, jnp.zeros_like(a1)], axis=1)
    all_places().wait_recv()

    def onto_next(c):
        cross_copy(c).wait_recv()
        along_copy(c).start()

    def onto_twin(c):
        along_copy(c).wait_recv()
        twin_copy(c).start()

    onto_next(first)
    onto_next(first + 1)
    for step in (0, 1, 3, 4):
        both, norm = spread(place_ref[step], step)
        put_right(both, norm, step)

    def left_of(g):
        return jnp.transpose(left_ref[g]).astype(BF16)

    def block_pair(left, g, n):
        right = jnp.concatenate([right_ref[column(g, n)], right_ref[column(g, n + 1)]], axis=1)
        right = jnp.concatenate([right, right], axis=0)
        square = jnp.dot(left, right, preferred_element_type=F32)
        square = jnp.maximum(square, 1e-10)
        rest = CUTOFF * LOG2E - square * lax.rsqrt(square)
        taper = jnp.maximum(rest, 0.0)
        return (jnp.exp2(rest) * taper * taper).astype(BF16)

    def build(g):
        left = left_of(g)
        for n in range(0, slots, 2):
            early_ref[g, :, n * BS : (n + 2) * BS] = block_pair(left, g, n)

    early = early_ref.shape[0]
    late = late_ref.shape[0]
    share = early // late
    paced = early - 5

    def upto(c):
        return (7 * c - 3 * ((c + 5) // 6)) // 2

    assert upto(0) == 0 and upto(main) == paced

    def turn(c, carry):
        def row(g, carry):
            build(g)
            return carry

        lax.fori_loop(upto(c), upto(c + 1), row, 0)
        onto_next(c)

        @pl.when(c == 1)
        def _():
            onto_twin(first)
            onto_twin(first + 1)

        @pl.when(c >= 2)
        def _():
            onto_twin(c - 2)

        return carry

    lax.fori_loop(0, main, turn, 0)
    onto_next(last)
    onto_next(last + 1)
    every(2, lambda j: build(paced + j))
    onto_twin(main - 2)
    every(3, lambda j: build(paced + 2 + j))
    for c in (main - 1, last, last + 1):
        onto_twin(c)
    own_copy().wait_recv()
    all_rows(twin_s, twin_r).wait_recv()

    factor = math.exp(-CUTOFF) / (8.0 * (CUTOFF * LOG2E) ** 2)

    def out_copy(g):
        return pltpu.make_async_copy(image_ref.at[g + 1], image_hbm.at[g], out_sem)

    def add_gram(image):
        high = image.astype(BF16)
        low = (image - high.astype(F32)).astype(BF16)
        pair = jnp.concatenate([high, low], axis=1)
        local_ref[...] += lax.dot_general(
            high, pair, (((0,), (0,)), ((), ())), preferred_element_type=F32
        )

    def multiply(g, source, at, beside):
        add_gram(image_ref[g])
        acc = jnp.zeros((BS, rank), F32)
        for n in range(0, slots, 2):
            parts = jnp.concatenate([wide_ref[column(g, n)], wide_ref[column(g, n + 1)]], axis=0)
            beside()
            acc = acc + jnp.dot(
                source[at, :, n * BS : (n + 2) * BS], parts, preferred_element_type=F32
            )
        image = acc * factor + NUGGET * own_ref[g].astype(F32)
        image_ref[g + 1] = image
        out_copy(g).start()

    def both_at_once(t):
        left = left_of(early + t)
        done = [0, 0]

        def beside():
            if done[0] % share == 0:
                n = 2 * done[1]
                late_ref[t, :, n * BS : (n + 2) * BS] = block_pair(left, early + t, n)
                done[1] += 1
            done[0] += 1

        for i in range(share):
            g = t * share + i
            multiply(g, early_ref, g, beside)

    every(late, both_at_once)
    every(late, lambda t: multiply(early + t, late_ref, t, lambda: None))
    add_gram(image_ref[rows])
    cross = local_ref[:, rank:]
    part = local_ref[:, :rank] + cross + jnp.transpose(cross)
    part_ref[...] = part.reshape(part_ref.shape)

    def copy1(k):
        p, device = peer_a(k)
        return remote(part_ref.at[p], got1.at[a], s1, r1, device)

    def copy2(k):
        return remote(one_sum, got2.at[y], s2, r2, peer_y(k))

    def copy3(k):
        return remote(two_sum, got3.at[z], s3, r3, peer_z(k))

    def copy4(k):
        return remote(three_sum, got4.at[a], s4, r4, peer_a(k)[1])

    def all_pieces(got, count, send, recv):
        pieces_of_others = got.at[pl.ds(0, count - 1)]
        return remote(pieces_of_others, pieces_of_others, send, recv, twin)

    def exchange(copy, count, own, value, got, send, recv):
        for k in range(1, count):
            copy(k).start()
        got[own] = value
        all_pieces(got, count, send, recv).wait_recv()

    exchange(copy1, 8, a, part_ref[a], got1, s1, r1)
    one_sum[...] = jnp.sum(got1[...], axis=0)
    exchange(copy2, 4, y, one_sum[...], got2, s2, r2)
    two_sum[...] = jnp.sum(got2[...], axis=0)
    exchange(copy3, 8, z, two_sum[...], got3, s3, r3)
    three_sum[...] = jnp.sum(got3[...], axis=0) * (1.0 / total)
    exchange(copy4, 8, a, three_sum[...], got4, s4, r4)
    gram_ref[...] = got4[...]

    pltpu.make_async_copy(image_ref.at[pl.ds(1, rows)], image_hbm, out_sem).wait()
    all_places().wait_send()
    own_copy().wait_send()
    for send in (cross_s, along_s, twin_s):
        all_rows(send, own_r).wait_send()
    for got, count, send, recv in (
        (got1, 8, s1, r1), (got2, 4, s2, r2), (got3, 8, s3, r3), (got4, 8, s4, r4),
    ):
        all_pieces(got, count, send, recv).wait_send()


def image_and_gram(near, ranges, coords, own, slabs, total):
    rows, size, rank = own.shape
    slots = near.shape[1]
    late = rows // 4
    early = rows - late
    vmem = pl.BlockSpec(memory_space=pltpu.VMEM)
    smem = pl.BlockSpec(memory_space=pltpu.SMEM)
    dma = pltpu.SemaphoreType.DMA
    piece = rank // 8
    image, gram = pl.pallas_call(
        functools.partial(image_kernel, total, slabs),
        name="image",
        out_shape=(
            jax.ShapeDtypeStruct((rows, size, rank), F32),
            jax.ShapeDtypeStruct((8, piece, rank), F32),
        ),
        in_specs=[smem, smem, vmem, vmem],
        out_specs=(pl.BlockSpec(memory_space=pl.ANY), vmem),
        scratch_shapes=[
            pltpu.VMEM((early, size, slots * size), BF16),
            pltpu.VMEM((late, size, slots * size), BF16),
            pltpu.VMEM((rows + 1, size, rank), F32),
            pltpu.VMEM((STEPS * rows, size, rank), BF16),
            pltpu.VMEM((STEPS, rows * 4, size), BF16),
            pltpu.VMEM((rows * 4, size), BF16),
            pltpu.VMEM((rows * 4, size), F32),
            pltpu.VMEM((STEPS * rows, 16, size), BF16),
            pltpu.VMEM((rows, 32, size), F32),
            pltpu.VMEM((rank, 2 * rank), F32),
        ]
        + [pltpu.VMEM((n, piece, rank), F32) for n in (8, 8, 4, 8, 8)]
        + [pltpu.VMEM((piece, rank), F32)] * 3
        + [dma(())] * 2
        + [dma(()), dma((10,))] * 2
        + [dma(())] * 12
        + [dma(())],
        compiler_params=pltpu.CompilerParams(
            collective_id=1, has_side_effects=True, vmem_limit_bytes=58 << 20
        ),
    )(near, ranges, coords, own)
    return image, gram.reshape(rank, rank)


def nt(a, b):
    return lax.dot_general(
        a, b, (((1,), (1,)), ((), ())), precision=HIGHEST, preferred_element_type=F32
    )


def nn(a, b):
    return jnp.dot(a, b, precision=HIGHEST, preferred_element_type=F32)


def basis_kernel(
    gram_ref, image_hbm, basis_hbm, factor_ref, inverse_ref, work_ref, image_ref, out_ref,
    in_sem, out_sem,
):
    n = gram_ref.shape[0]
    chunks = out_sem.shape[0]
    size = image_ref.shape[0] // chunks
    fetch = pltpu.make_async_copy(image_hbm, image_ref, in_sem)
    fetch.start()

    row = lax.broadcasted_iota(jnp.int32, (n, n), 0)
    col = lax.broadcasted_iota(jnp.int32, (n, n), 1)
    diag = row == col
    weight = jnp.where(row > col, 1.0, jnp.where(diag, 0.5, 0.0)).astype(F32)
    eye = jnp.where(diag, 1.0, 0.0).astype(F32)
    gram = gram_ref[...]
    only = jnp.where(diag, gram, 0.0)
    down = lax.rsqrt(jnp.sum(only, axis=1, keepdims=True))
    across = lax.rsqrt(jnp.sum(only, axis=0, keepdims=True))
    first = gram * down * across - eye
    inverse_ref[...] = (eye - first * weight) * across

    def unsettled(state):
        size, turn = state
        return jnp.logical_and(jnp.logical_not(size < 1e-6), turn < 8)

    def refine(state):
        turn = state[1]
        x = inverse_ref[...]
        gap = nt(nn(x, gram_ref[...]), x) - eye
        inverse_ref[...] = x - nn(gap * weight, x)
        return jnp.sum(gap * gap), turn + 1

    far, _ = lax.while_loop(unsettled, refine, (jnp.sum(first * first), jnp.int32(0)))
    settled = far < 1e-6

    @pl.when(settled)
    def _():
        factor_ref[...] = jnp.where(row <= col, nn(inverse_ref[...], gram_ref[...]), 0.0)

    @pl.when(jnp.logical_not(settled))
    def _():
        work_ref[:, :n] = gram_ref[...]
        work_ref[:, n:] = eye
        wide = lax.broadcasted_iota(jnp.int32, (n, 2 * n), 1)
        tall = lax.broadcasted_iota(jnp.int32, (n, 1), 0)

        def eliminate(k, c):
            m = work_ref[...]
            pivot_row = jnp.sum(jnp.where(tall == k, m, 0.0), axis=0, keepdims=True)
            column = jnp.sum(jnp.where(wide == k, m, 0.0), axis=1, keepdims=True)
            pivot = jnp.sum(jnp.where(tall == k, column, 0.0), axis=0, keepdims=True)
            ratio = jnp.where(tall > k, column / pivot, 0.0)
            work_ref[...] = m - ratio * pivot_row
            return c

        lax.fori_loop(0, n, eliminate, 0)
        upper = work_ref[:, :n]
        scale = lax.rsqrt(jnp.sum(jnp.where(diag, upper, 0.0), axis=1, keepdims=True))
        factor_ref[...] = jnp.where(row <= col, upper * scale, 0.0)
        inverse_ref[...] = work_ref[:, n:] * scale

    x = jnp.transpose(inverse_ref[...])
    xh = x.astype(BF16)
    xl = (x - xh.astype(F32)).astype(BF16)
    right = jnp.concatenate(
        [
            jnp.concatenate([xh, xl], axis=1),
            jnp.concatenate([xh, jnp.zeros_like(xl)], axis=1),
        ],
        axis=0,
    )
    fetch.wait()

    def send(i):
        piece = pl.ds(i * size, size)
        return pltpu.make_async_copy(out_ref.at[piece], basis_hbm.at[piece], out_sem.at[i])

    for i in range(chunks):
        image = image_ref[i * size : (i + 1) * size]
        high = image.astype(BF16)
        low = (image - high.astype(F32)).astype(BF16)
        both = jnp.concatenate([high, low], axis=1)
        product = jnp.dot(both, right, preferred_element_type=F32)
        out_ref[i * size : (i + 1) * size] = product[:, :n] + product[:, n:]
        send(i).start()
    for i in range(chunks):
        send(i).wait()


def basis_and_factor(gram, image):
    n = gram.shape[0]
    rows = image.shape[0]
    chunks = 8
    vmem = pl.BlockSpec(memory_space=pltpu.VMEM)
    hbm = pl.BlockSpec(memory_space=pl.ANY)
    return pl.pallas_call(
        basis_kernel,
        name="basis",
        out_shape=(
            jax.ShapeDtypeStruct((rows, n), F32),
            jax.ShapeDtypeStruct((n, n), F32),
        ),
        in_specs=[vmem, hbm],
        out_specs=(hbm, vmem),
        scratch_shapes=[
            pltpu.VMEM((n, n), F32),
            pltpu.VMEM((n, 2 * n), F32),
            pltpu.VMEM((rows, n), F32),
            pltpu.VMEM((rows, n), F32),
            pltpu.SemaphoreType.DMA(()),
            pltpu.SemaphoreType.DMA((chunks,)),
        ],
    )(gram, image)


def on_device(panel, coords, neighbours, ranges):
    block_count = neighbours.shape[0]
    block_size = panel.shape[0] // block_count
    width = panel.shape[1]
    sector_count = lax.axis_size("sector")
    slab_count = lax.axis_size("depth")
    blocked = panel.reshape(block_count, block_size, width)

    total_cells = float(panel.shape[0] * sector_count * slab_count)
    image, gram = image_and_gram(
        neighbours, ranges, coords, blocked, slab_count, total_cells
    )
    image = image.reshape(block_count * block_size, width)
    basis, factor = basis_and_factor(gram, image)
    return (basis, factor)


def solution(mesh):
    in_specs = (
        P(("sector", "depth"), None),
        P(None, ("sector", "depth")),
        P(("sector", "depth"), None),
        P(),
    )
    out_specs = (P(("sector", "depth"), None), P())
    return jax.shard_map(
        on_device, mesh=mesh, in_specs=in_specs, out_specs=out_specs, check_vma=False
    )
```

```python
import functools
import math

import jax
import jax.numpy as jnp
from jax import lax
from jax.experimental import pallas as pl
from jax.experimental.pallas import tpu as pltpu
from jax.sharding import PartitionSpec as P

AZ_SEC = 8
DZ = 8
CUTOFF = 3.0
NUGGET = 0.5
BS = 128
LOG2E = 1.4426950408889634
MESH = pl.DeviceIdType.MESH
F32 = jnp.float32
BF16 = jnp.bfloat16
HIGHEST = lax.Precision.HIGHEST


STEPS = 5


def place():
    s = lax.axis_index("sector")
    d = lax.axis_index("depth")
    return s // 4, (s // 2) % 2, s % 2, d // 8, d % 8


def short(value):
    return value.astype(BF16).astype(F32)


def pieces(value):
    one = short(value)
    two = short(value - one)
    return one, two, value - one - two


def image_kernel(
    total, slabs, near, ranges, coords_ref, own_ref, image_hbm, gram_ref,
    early_ref, late_ref, image_ref, wide_ref, place_ref, mine_ref, point_ref, right_ref, left_ref, local_ref,
    part_ref, got1, got2, got3, got4, one_sum, two_sum, three_sum,
    place_s, place_r, cross_s, cross_r, along_s, along_r, twin_s, twin_r, own_s, own_r,
    s1, r1, s2, r2, s3, r3, s4, r4, out_sem,
):
    rows, rank = own_ref.shape[0], own_ref.shape[2]
    slots = near.shape[1]
    size = rows // 8
    half = size // 2
    main = 6
    first, last = main, main + 2
    spans = {first: 0, first + 1: half, last: rows - size, last + 1: rows - half}
    y, xh, core, xl, z = place()
    s = lax.axis_index("sector")
    d = lax.axis_index("depth")
    x = xh * 2 + xl
    a = core * 4 + x

    def sector(k):
        return lax.rem(s + k + 16, 16), d

    def peer_a(k):
        p = lax.rem(a + k, 8)
        px = lax.rem(p, 4)
        return p, (y * 4 + (px // 2) * 2 + p // 4, lax.rem(px, 2) * 8 + z)

    def peer_y(k):
        return lax.rem(s + 4 * k, 16), d

    def peer_z(k):
        return s, xl * 8 + lax.rem(z + k, 8)

    barrier = pltpu.get_barrier_semaphore()
    greeted = [sector(k) for k in (-2, -1, 1, 2)]
    greeted += [peer_y(k) for k in range(1, 4)]
    greeted += [peer_a(k)[1] for k in range(1, 8)] + [peer_z(k) for k in range(1, 8)]
    for device in greeted:
        pl.semaphore_signal(barrier, inc=1, device_id=device, device_id_type=MESH)

    corner = lax.broadcasted_iota(jnp.int32, (3, 1), 0)
    corner = jnp.where(corner == 0, s * AZ_SEC, jnp.where(corner == 1, 32, d * DZ + DZ // 2))
    point_ref[...] = jnp.ones_like(point_ref)
    for g in range(rows):
        inside = coords_ref[:, g * BS : (g + 1) * BS] - corner
        point_ref[4 * g : 4 * g + 3, :] = inside.astype(F32)
    mine_ref[...] = point_ref[...].astype(BF16)

    shift = (slabs * rows).bit_length() - 1

    def column(g, n):
        block = near[g, n]
        step = lax.rem(lax.shift_right_logical(block, shift) - s + 18, 16)
        return jnp.minimum(step, STEPS - 1) * rows + lax.rem(block, rows)

    pl.semaphore_wait(barrier, len(greeted))

    opposite = sector(2 - 4 * xh)
    onward = sector(4 - 8 * xh)
    across_at = (4 - 4 * xh) * rows
    along_at = 4 * xh * rows
    twin = sector(1 - 2 * core)
    twin_from = (4 - 4 * core) * rows
    twin_to = (3 - 2 * core) * rows
    own_to = (1 + 2 * core) * rows

    def remote(src, dst, send, recv, dev):
        return pltpu.make_async_remote_copy(
            src, dst, send, recv, device_id=dev, device_id_type=MESH
        )

    def place_copy(i):
        k = (-2, -1, 1, 2)[i]
        return remote(mine_ref, place_ref.at[2 - k], place_s, place_r, sector(k))

    def all_places():
        four = place_ref.at[pl.ds(0, 4)]
        return remote(four, four, place_s, place_r, twin)

    def all_rows(send, recv):
        whole = wide_ref.at[pl.ds(0, rows)]
        return remote(whole, whole, send, recv, twin)

    def span(c):
        return (spans[c], half) if isinstance(c, int) and c >= main else (size + c * size, size)

    def cross_copy(c):
        start, count = span(c)
        return remote(
            own_ref.at[pl.ds(start, count)],
            wide_ref.at[pl.ds(4 * xh * rows + start, count)],
            cross_s, cross_r.at[c], opposite,
        )

    def along_copy(c):
        start, count = span(c)
        return remote(
            wide_ref.at[pl.ds(across_at + start, count)],
            wide_ref.at[pl.ds(along_at + start, count)],
            along_s, along_r.at[c], onward,
        )

    def twin_copy(c):
        start, count = span(c)
        return remote(
            wide_ref.at[pl.ds(twin_from + start, count)],
            wide_ref.at[pl.ds(twin_to + start, count)],
            twin_s, twin_r, twin,
        )

    def own_copy():
        return remote(own_ref, wide_ref.at[pl.ds(own_to, rows)], own_s, own_r, twin)

    def every(count, do):
        def step(k, c):
            do(k)
            return c

        lax.fori_loop(0, count, step, 0)

    for i in range(4):
        place_copy(i).start()
    for c in (first, first + 1, 0, 1):
        cross_copy(c).start()
    own_copy().start()
    wide_ref[pl.ds(2 * rows, rows)] = own_ref[...]
    local_ref[...] = jnp.zeros_like(local_ref)
    image_ref[0] = jnp.zeros((BS, rank), F32)

    line = lax.broadcasted_iota(jnp.int32, (1, 8, BS), 1)
    w = jnp.where(line == 0, ranges[0], jnp.where(line == 1, ranges[1], ranges[2]))
    w = LOG2E / w
    w = jnp.where(line < 3, w * w, 0.0)

    def spread(ref_value, step):
        even = ref_value.astype(F32).reshape(rows // 2, 8, BS)
        odd = jnp.concatenate([even[:, 4:], even[:, :4]], axis=1)
        both = jnp.stack([even, odd], axis=1).reshape(rows, 8, BS)
        both = both + jnp.where(line == 0, 8.0 * (step - 2) - 4.0, 0.0)
        norm = jnp.sum(both * both * w, axis=1, keepdims=True)
        return both, norm

    def put_right(both, norm, step):
        n1, n2, n3 = pieces(norm)
        tail = jnp.where(line == 4, n1, jnp.where(line == 5, n2, jnp.where(line == 6, n3, 0.0)))
        base = jnp.where(line < 4, both, tail)
        twice = jnp.concatenate([base, base], axis=1).astype(BF16)
        right_ref[pl.ds(step * rows, rows)] = twice

    both, norm = spread(point_ref[...], 2)
    put_right(both, norm, 2)
    full = jnp.where(line < 3, -2.0 * w * both, jnp.where(line == 3, norm, 0.0))
    a1, a2, a3 = pieces(full)
    a1 = a1 + jnp.where(jnp.logical_and(line > 3, line < 7), 1.0, 0.0)
    left_ref[...] = jnp.concatenate([a1, a2, a3, jnp.zeros_like(a1)], axis=1)
    all_places().wait_recv()

    def onto_next(c):
        cross_copy(c).wait_recv()
        along_copy(c).start()

    def onto_twin(c):
        along_copy(c).wait_recv()
        twin_copy(c).start()

    onto_next(first)
    cross_copy(2).start()
    onto_next(first + 1)
    cross_copy(3).start()
    for step in (0, 1, 3, 4):
        both, norm = spread(place_ref[step], step)
        put_right(both, norm, step)

    def left_of(g):
        return jnp.transpose(left_ref[g]).astype(BF16)

    def block_pair(left, g, n):
        right = jnp.concatenate([right_ref[column(g, n)], right_ref[column(g, n + 1)]], axis=1)
        right = jnp.concatenate([right, right], axis=0)
        square = jnp.dot(left, right, preferred_element_type=F32)
        square = jnp.maximum(square, 1e-10)
        rest = CUTOFF * LOG2E - square * lax.rsqrt(square)
        taper = jnp.maximum(rest, 0.0)
        return (jnp.exp2(rest) * taper * taper).astype(BF16)

    def build(g):
        left = left_of(g)
        for n in range(0, slots, 2):
            early_ref[g, :, n * BS : (n + 2) * BS] = block_pair(left, g, n)

    early = early_ref.shape[0]
    late = late_ref.shape[0]
    share = early // late
    paced = early - 5

    def upto(c):
        return (7 * c - 3 * ((c + 5) // 6)) // 2

    assert upto(0) == 0 and upto(main) == paced

    def turn(c, carry):
        def row(g, carry):
            build(g)
            return carry

        lax.fori_loop(upto(c), upto(c + 1), row, 0)
        onto_next(c)

        @pl.when(c < 2)
        def _():
            cross_copy(c + 4).start()

        @pl.when(c == 2)
        def _():
            cross_copy(last).start()

        @pl.when(c == 3)
        def _():
            cross_copy(last + 1).start()

        @pl.when(c == 1)
        def _():
            onto_twin(first)
            onto_twin(first + 1)

        @pl.when(c >= 2)
        def _():
            onto_twin(c - 2)

        return carry

    lax.fori_loop(0, main, turn, 0)
    onto_next(last)
    onto_next(last + 1)
    every(2, lambda j: build(paced + j))
    onto_twin(main - 2)
    every(3, lambda j: build(paced + 2 + j))
    for c in (main - 1, last, last + 1):
        onto_twin(c)
    own_copy().wait_recv()
    all_rows(twin_s, twin_r).wait_recv()

    factor = math.exp(-CUTOFF) / (8.0 * (CUTOFF * LOG2E) ** 2)

    def out_copy(g):
        return pltpu.make_async_copy(image_ref.at[g + 1], image_hbm.at[g], out_sem)

    def add_gram(image):
        high = image.astype(BF16)
        low = (image - high.astype(F32)).astype(BF16)
        pair = jnp.concatenate([high, low], axis=1)
        local_ref[...] += lax.dot_general(
            high, pair, (((0,), (0,)), ((), ())), preferred_element_type=F32
        )

    def multiply(g, source, at, beside):
        add_gram(image_ref[g])
        acc = jnp.zeros((BS, rank), F32)
        for n in range(0, slots, 2):
            parts = jnp.concatenate([wide_ref[column(g, n)], wide_ref[column(g, n + 1)]], axis=0)
            beside()
            acc = acc + jnp.dot(
                source[at, :, n * BS : (n + 2) * BS], parts, preferred_element_type=F32
            )
        image = acc * factor + NUGGET * own_ref[g].astype(F32)
        image_ref[g + 1] = image
        out_copy(g).start()

    def both_at_once(t):
        left = left_of(early + t)
        done = [0, 0]

        def beside():
            if done[0] % share == 0:
                n = 2 * done[1]
                late_ref[t, :, n * BS : (n + 2) * BS] = block_pair(left, early + t, n)
                done[1] += 1
            done[0] += 1

        for i in range(share):
            g = t * share + i
            multiply(g, early_ref, g, beside)

    every(late, both_at_once)
    every(late, lambda t: multiply(early + t, late_ref, t, lambda: None))
    add_gram(image_ref[rows])
    cross = local_ref[:, rank:]
    part = local_ref[:, :rank] + cross + jnp.transpose(cross)
    part_ref[...] = part.reshape(part_ref.shape)

    def copy1(k):
        p, device = peer_a(k)
        return remote(part_ref.at[p], got1.at[a], s1, r1, device)

    def copy2(k):
        return remote(one_sum, got2.at[y], s2, r2, peer_y(k))

    def copy3(k):
        return remote(two_sum, got3.at[z], s3, r3, peer_z(k))

    def copy4(k):
        return remote(three_sum, got4.at[a], s4, r4, peer_a(k)[1])

    def all_pieces(got, count, send, recv):
        pieces_of_others = got.at[pl.ds(0, count - 1)]
        return remote(pieces_of_others, pieces_of_others, send, recv, twin)

    def exchange(copy, count, own, value, got, send, recv):
        for k in range(1, count):
            copy(k).start()
        got[own] = value
        all_pieces(got, count, send, recv).wait_recv()

    exchange(copy1, 8, a, part_ref[a], got1, s1, r1)
    one_sum[...] = jnp.sum(got1[...], axis=0)
    exchange(copy2, 4, y, one_sum[...], got2, s2, r2)
    two_sum[...] = jnp.sum(got2[...], axis=0)
    exchange(copy3, 8, z, two_sum[...], got3, s3, r3)
    three_sum[...] = jnp.sum(got3[...], axis=0) * (1.0 / total)
    exchange(copy4, 8, a, three_sum[...], got4, s4, r4)
    gram_ref[...] = got4[...]

    pltpu.make_async_copy(image_ref.at[pl.ds(1, rows)], image_hbm, out_sem).wait()
    all_places().wait_send()
    own_copy().wait_send()
    for send in (cross_s, along_s, twin_s):
        all_rows(send, own_r).wait_send()
    for got, count, send, recv in (
        (got1, 8, s1, r1), (got2, 4, s2, r2), (got3, 8, s3, r3), (got4, 8, s4, r4),
    ):
        all_pieces(got, count, send, recv).wait_send()


def image_and_gram(near, ranges, coords, own, slabs, total):
    rows, size, rank = own.shape
    slots = near.shape[1]
    late = rows // 4
    early = rows - late
    vmem = pl.BlockSpec(memory_space=pltpu.VMEM)
    smem = pl.BlockSpec(memory_space=pltpu.SMEM)
    dma = pltpu.SemaphoreType.DMA
    piece = rank // 8
    image, gram = pl.pallas_call(
        functools.partial(image_kernel, total, slabs),
        name="image",
        out_shape=(
            jax.ShapeDtypeStruct((rows, size, rank), F32),
            jax.ShapeDtypeStruct((8, piece, rank), F32),
        ),
        in_specs=[smem, smem, vmem, vmem],
        out_specs=(pl.BlockSpec(memory_space=pl.ANY), vmem),
        scratch_shapes=[
            pltpu.VMEM((early, size, slots * size), BF16),
            pltpu.VMEM((late, size, slots * size), BF16),
            pltpu.VMEM((rows + 1, size, rank), F32),
            pltpu.VMEM((STEPS * rows, size, rank), BF16),
            pltpu.VMEM((STEPS, rows * 4, size), BF16),
            pltpu.VMEM((rows * 4, size), BF16),
            pltpu.VMEM((rows * 4, size), F32),
            pltpu.VMEM((STEPS * rows, 16, size), BF16),
            pltpu.VMEM((rows, 32, size), F32),
            pltpu.VMEM((rank, 2 * rank), F32),
        ]
        + [pltpu.VMEM((n, piece, rank), F32) for n in (8, 8, 4, 8, 8)]
        + [pltpu.VMEM((piece, rank), F32)] * 3
        + [dma(())] * 2
        + [dma(()), dma((10,))] * 2
        + [dma(())] * 12
        + [dma(())],
        compiler_params=pltpu.CompilerParams(
            collective_id=1, has_side_effects=True, vmem_limit_bytes=58 << 20
        ),
    )(near, ranges, coords, own)
    return image, gram.reshape(rank, rank)


def nt(a, b):
    return lax.dot_general(
        a, b, (((1,), (1,)), ((), ())), precision=HIGHEST, preferred_element_type=F32
    )


def nn(a, b):
    return jnp.dot(a, b, precision=HIGHEST, preferred_element_type=F32)


def basis_kernel(
    gram_ref, image_hbm, basis_hbm, factor_ref, inverse_ref, work_ref, image_ref, out_ref,
    in_sem, out_sem,
):
    n = gram_ref.shape[0]
    chunks = out_sem.shape[0]
    size = image_ref.shape[0] // chunks
    fetch = pltpu.make_async_copy(image_hbm, image_ref, in_sem)
    fetch.start()

    row = lax.broadcasted_iota(jnp.int32, (n, n), 0)
    col = lax.broadcasted_iota(jnp.int32, (n, n), 1)
    diag = row == col
    weight = jnp.where(row > col, 1.0, jnp.where(diag, 0.5, 0.0)).astype(F32)
    eye = jnp.where(diag, 1.0, 0.0).astype(F32)
    gram = gram_ref[...]
    only = jnp.where(diag, gram, 0.0)
    down = lax.rsqrt(jnp.sum(only, axis=1, keepdims=True))
    across = lax.rsqrt(jnp.sum(only, axis=0, keepdims=True))
    first = gram * down * across - eye
    inverse_ref[...] = (eye - first * weight) * across

    def unsettled(state):
        size, turn = state
        return jnp.logical_and(jnp.logical_not(size < 1e-6), turn < 8)

    def refine(state):
        turn = state[1]
        x = inverse_ref[...]
        gap = nt(nn(x, gram_ref[...]), x) - eye
        inverse_ref[...] = x - nn(gap * weight, x)
        return jnp.sum(gap * gap), turn + 1

    far, _ = lax.while_loop(unsettled, refine, (jnp.sum(first * first), jnp.int32(0)))
    settled = far < 1e-6

    @pl.when(settled)
    def _():
        factor_ref[...] = jnp.where(row <= col, nn(inverse_ref[...], gram_ref[...]), 0.0)

    @pl.when(jnp.logical_not(settled))
    def _():
        work_ref[:, :n] = gram_ref[...]
        work_ref[:, n:] = eye
        wide = lax.broadcasted_iota(jnp.int32, (n, 2 * n), 1)
        tall = lax.broadcasted_iota(jnp.int32, (n, 1), 0)

        def eliminate(k, c):
            m = work_ref[...]
            pivot_row = jnp.sum(jnp.where(tall == k, m, 0.0), axis=0, keepdims=True)
            column = jnp.sum(jnp.where(wide == k, m, 0.0), axis=1, keepdims=True)
            pivot = jnp.sum(jnp.where(tall == k, column, 0.0), axis=0, keepdims=True)
            ratio = jnp.where(tall > k, column / pivot, 0.0)
            work_ref[...] = m - ratio * pivot_row
            return c

        lax.fori_loop(0, n, eliminate, 0)
        upper = work_ref[:, :n]
        scale = lax.rsqrt(jnp.sum(jnp.where(diag, upper, 0.0), axis=1, keepdims=True))
        factor_ref[...] = jnp.where(row <= col, upper * scale, 0.0)
        inverse_ref[...] = work_ref[:, n:] * scale

    x = jnp.transpose(inverse_ref[...])
    xh = x.astype(BF16)
    xl = (x - xh.astype(F32)).astype(BF16)
    right = jnp.concatenate(
        [
            jnp.concatenate([xh, xl], axis=1),
            jnp.concatenate([xh, jnp.zeros_like(xl)], axis=1),
        ],
        axis=0,
    )
    fetch.wait()

    def send(i):
        piece = pl.ds(i * size, size)
        return pltpu.make_async_copy(out_ref.at[piece], basis_hbm.at[piece], out_sem.at[i])

    for i in range(chunks):
        image = image_ref[i * size : (i + 1) * size]
        high = image.astype(BF16)
        low = (image - high.astype(F32)).astype(BF16)
        both = jnp.concatenate([high, low], axis=1)
        product = jnp.dot(both, right, preferred_element_type=F32)
        out_ref[i * size : (i + 1) * size] = product[:, :n] + product[:, n:]
        send(i).start()
    for i in range(chunks):
        send(i).wait()


def basis_and_factor(gram, image):
    n = gram.shape[0]
    rows = image.shape[0]
    chunks = 8
    vmem = pl.BlockSpec(memory_space=pltpu.VMEM)
    hbm = pl.BlockSpec(memory_space=pl.ANY)
    return pl.pallas_call(
        basis_kernel,
        name="basis",
        out_shape=(
            jax.ShapeDtypeStruct((rows, n), F32),
            jax.ShapeDtypeStruct((n, n), F32),
        ),
        in_specs=[vmem, hbm],
        out_specs=(hbm, vmem),
        scratch_shapes=[
            pltpu.VMEM((n, n), F32),
            pltpu.VMEM((n, 2 * n), F32),
            pltpu.VMEM((rows, n), F32),
            pltpu.VMEM((rows, n), F32),
            pltpu.SemaphoreType.DMA(()),
            pltpu.SemaphoreType.DMA((chunks,)),
        ],
    )(gram, image)


def on_device(panel, coords, neighbours, ranges):
    block_count = neighbours.shape[0]
    block_size = panel.shape[0] // block_count
    width = panel.shape[1]
    sector_count = lax.axis_size("sector")
    slab_count = lax.axis_size("depth")
    blocked = panel.reshape(block_count, block_size, width)

    total_cells = float(panel.shape[0] * sector_count * slab_count)
    image, gram = image_and_gram(
        neighbours, ranges, coords, blocked, slab_count, total_cells
    )
    image = image.reshape(block_count * block_size, width)
    basis, factor = basis_and_factor(gram, image)
    return (basis, factor)


def solution(mesh):
    in_specs = (
        P(("sector", "depth"), None),
        P(None, ("sector", "depth")),
        P(("sector", "depth"), None),
        P(),
    )
    out_specs = (P(("sector", "depth"), None), P())
    return jax.shard_map(
        on_device, mesh=mesh, in_specs=in_specs, out_specs=out_specs, check_vma=False
    )
```
